256 devices in a mesh: seq: 64 (over z_hi, y, x, core), chan: 4 (over z_lo).
Axes of the slice: x: 4, y: 4, z: 8 (z_hi: 2, z_lo: 4; z = z_hi * 4 + z_lo), core: 2. Of those that a mesh axis runs over, the one named last changes fastest.
Arguments:
- layer_input: bfloat16 [8192, 4096], P('seq', 'chan'), may hold values from -16 to 16
- gate_query: bfloat16 [8192, 4096], P('seq', 'chan'), may hold values from -6 to 6
- gate_key: bfloat16 [8192, 4096], P('seq', 'chan'), may hold values from -6 to 6
- value_proj: bfloat16 [8192, 4096], P('seq', 'chan'), may hold values from -6 to 6
- grad_out: bfloat16 [8192, 4096], P('seq', 'chan'), may hold values from -6 to 6
- filter_taps: bfloat16 [8192, 4096], P('seq', 'chan'), may hold values from -1.1 to 1.1
Outputs:
- grad_query: bfloat16 [8192, 4096], P('seq', 'chan')
- grad_key: bfloat16 [8192, 4096], P('seq', 'chan')
- grad_value: bfloat16 [8192, 4096], P('seq', 'chan')
- grad_filter: bfloat16 [8192, 4096], P('seq', 'chan')
- grad_weight: float32 [4096, 4096], P('seq', 'chan')
The draws below stay inside these ranges and needn't reach their ends.
All inputs are finite; a program needn't handle non-finite values.
Results may differ from the reference program's by a relative error of at most 0.0067.
Values may be sent and summed in bfloat16 or wider, within the bound.
No kernel may reach another device: no remote copies, remote signals or barrier semaphores. Data moves between devices by JAX's collectives and lax.ppermute only.
A program may use at most 128 MiB of HBM per device.

```python
import math
import jax
import jax.numpy as jnp
from jax import lax

D = 4096
P_SIZE = 128
LENGTH = 8192


def draw_filter_taps(key, part):
    first, second = jax.random.split(jax.random.fold_in(key, 17))
    rates = jax.random.uniform(first, (1, D), minval=math.log(30.0), maxval=math.log(4.0 * LENGTH))
    noise = jnp.clip(jax.random.normal(second, (LENGTH, D)), -4.0, 4.0)
    spans = jnp.exp(rates)
    places = jnp.arange(LENGTH, dtype=jnp.float32)[:, None]
    kept = jnp.minimum(spans, float(LENGTH))
    taps = noise * jnp.exp(-places / spans) * jnp.sqrt(2.0 / kept)
    return taps.astype(jnp.float32).astype(jnp.bfloat16)


def strengthened(values, stream_key, source, target, shards_of, factor):
    def block_of(position):
        return (jnp.arange(values.shape[position]) // (values.shape[position] // shards_of)).reshape((-1,) + (1,) * (values.ndim - 1 - position))

    near = jax.random.permutation(stream_key, shards_of)[block_of(target)]
    far = (block_of(target) + shards_of // 2) % shards_of
    return jnp.where((block_of(source) == near) | (block_of(source) == far), factor * values, values)


def shard_levels(stream_key, extent, cuts, smallest, largest):
    gain, own = 1.0, jax.random.fold_in(stream_key, 6)
    for position, shards_of in cuts:
        steps = jnp.exp(jax.random.uniform(jax.random.fold_in(own, position), (shards_of,), jnp.float32, smallest / len(cuts), largest / len(cuts)))
        gain = gain * jnp.repeat(steps, extent[position] // shards_of).reshape([-1 if axis == position else 1 for axis in range(len(extent))])
    return gain


def gaussian(rng, dims, scale, most, cuts=(), kind=jnp.bfloat16):
    drawn = scale * jax.random.normal(rng, dims, jnp.float32)
    if cuts:
        drawn = drawn * shard_levels(rng, dims, cuts, -0.22, 0.18)
    return jnp.clip(drawn, -most, most).astype(kind)


def gaussian_with(own_key, extent, scale, limit, cuts, heavy, kind=jnp.bfloat16):
    values = scale * jax.random.normal(own_key, extent, jnp.float32)
    if cuts:
        values = values * shard_levels(own_key, extent, cuts, -0.22, 0.18)
    return jnp.clip(strengthened(values, jax.random.fold_in(own_key, 3), *heavy), -limit, limit).astype(kind)


def setup_inputs(seed: int = 0) -> dict:
    streams_of = jax.random.split(jax.random.key(seed), 7)
    return {
        "layer_input": gaussian_with(streams_of[0], (LENGTH, D), 1.0, 16.0, ((0, 64), (1, 4)), (0, 1, 64, 4.0)),
        "gate_query": gaussian(streams_of[1], (LENGTH, D), 1.0, 6.0, ((0, 64), (1, 4))),
        "gate_key": gaussian(streams_of[2], (LENGTH, D), 1.0, 6.0, ((0, 64), (1, 4))),
        "value_proj": gaussian(streams_of[3], (LENGTH, D), 1.0, 6.0, ((0, 64), (1, 4))),
        "grad_out": gaussian(streams_of[4], (LENGTH, D), 1.0, 6.0, ((0, 64), (1, 4))),
        "filter_taps": draw_filter_taps(jax.random.fold_in(streams_of[6], 71), 0),
    }


def angle_grid(first, second, period):
    product = first[:, None] * second[None, :] % period
    return product.astype(jnp.float32) * (2.0 * math.pi / period)

def round_back(array):
    return lax.optimization_barrier(array.astype(jnp.bfloat16)).astype(jnp.float32)

def transform(signal):
    blocks = LENGTH // P_SIZE
    width = signal.shape[1]
    shaped = signal.astype(jnp.float32).reshape(blocks, P_SIZE, width)
    padded = jnp.concatenate([shaped, jnp.zeros_like(shaped)], axis=0)
    across = jnp.fft.fft(padded, axis=0)
    angle = angle_grid(jnp.arange(2 * blocks, dtype=jnp.int32), jnp.arange(P_SIZE, dtype=jnp.int32), 2 * LENGTH)
    turned = across * lax.complex(jnp.cos(angle), -jnp.sin(angle))[:, :, None]
    real_part = round_back(jnp.real(turned))
    other_part = round_back(jnp.imag(turned))
    return jnp.fft.fft(lax.complex(real_part, other_part), axis=1)

def untransform(spectrum, factor):
    blocks = LENGTH // P_SIZE
    width = spectrum.shape[2]
    within = jnp.fft.ifft(spectrum, axis=1) * P_SIZE
    angle = angle_grid(jnp.arange(2 * blocks, dtype=jnp.int32), jnp.arange(P_SIZE, dtype=jnp.int32), 2 * LENGTH)
    turned = within * lax.complex(jnp.cos(angle), jnp.sin(angle))[:, :, None]
    real_part = round_back(jnp.real(turned))
    other_part = round_back(jnp.imag(turned))
    across = jnp.fft.ifft(lax.complex(real_part, other_part), axis=0) * (2 * blocks)
    return (jnp.real(across[:blocks]) * factor).reshape(LENGTH, width).astype(jnp.bfloat16)

def channel_block(pieces):
    mixed, taps, gated = pieces
    mixed_spec = transform(mixed)
    taps_spec = transform(taps)
    gated_spec = transform(gated)
    scale = 1.0 / (2 * LENGTH)
    conv_out = untransform(mixed_spec * taps_spec, scale)
    back_grad = untransform(gated_spec * jnp.conj(taps_spec), scale)
    grad_filter = untransform(gated_spec * jnp.conj(mixed_spec), scale / math.sqrt(LENGTH))
    return (conv_out, back_grad, grad_filter)

def reference(layer_input, gate_query, gate_key, value_proj, grad_out, filter_taps):
    mixed = (gate_key.astype(jnp.float32) * value_proj.astype(jnp.float32)).astype(jnp.bfloat16)
    gated = (grad_out.astype(jnp.float32) * gate_query.astype(jnp.float32)).astype(jnp.bfloat16)
    group = math.gcd(D, 512)
    number = D // group

    def split_channels(array):
        return array.reshape(LENGTH, number, group).transpose(1, 0, 2)

    def join_channels(array):
        return array.transpose(1, 0, 2).reshape(LENGTH, D)
    conv_out, back_grad, grad_filter = lax.map(channel_block, (split_channels(mixed), split_channels(filter_taps), split_channels(gated)))
    conv_out = join_channels(conv_out)
    back_grad = join_channels(back_grad)
    grad_filter = join_channels(grad_filter)
    grad_query = (grad_out.astype(jnp.float32) * conv_out.astype(jnp.float32)).astype(jnp.bfloat16)
    grad_key = (back_grad.astype(jnp.float32) * value_proj.astype(jnp.float32)).astype(jnp.bfloat16)
    grad_value = (back_grad.astype(jnp.float32) * gate_key.astype(jnp.float32)).astype(jnp.bfloat16)
    grad_weight = jnp.dot(layer_input.T, grad_value, preferred_element_type=jnp.float32) * (1.0 / math.sqrt(LENGTH))
    return (grad_query, grad_key, grad_value, grad_filter, grad_weight)
```

```python
import math

import numpy as np

import jax
import jax.numpy as jnp
from jax import lax
from jax.experimental import pallas as pl
from jax.experimental.pallas import tpu as pltpu
from jax.sharding import PartitionSpec as P

BLOCKS = 64
ROWS = 128
CHANNELS = 16
LANES = 3 * CHANNELS
PERIOD = 2 * BLOCKS * ROWS
LAST_SCALE = 1.0 / PERIOD
ROOT_SCALE = 1.0 / math.sqrt(BLOCKS * ROWS)
NEAR = [[8 * g + i for i in range(8)] for g in range(8)]
FAR = [[g + 8 * i for i in range(8)] for g in range(8)]


def split_table(table):
    high = table.astype(jnp.bfloat16)
    low = (table - high.astype(np.float64)).astype(jnp.bfloat16)
    return high, low


def make_tables():
    freq = np.arange(2 * BLOCKS)
    block = np.arange(BLOCKS)
    row = np.arange(ROWS)
    outer = 2.0 * math.pi * (freq[:, None] * block[None, :] % (2 * BLOCKS)) / (2 * BLOCKS)
    first = np.concatenate([np.cos(outer), -np.sin(outer)], axis=0)
    first = np.concatenate(split_table(first), axis=1)
    last = np.concatenate([np.cos(outer).T, -np.sin(outer).T], axis=1)
    last = np.concatenate(split_table(last), axis=0)
    twist = 2.0 * math.pi * (freq[:, None] * row[None, :] % PERIOD) / PERIOD
    inner = 2.0 * math.pi * (row[:, None] * row[None, :] % ROWS) / ROWS
    cosine, sine = np.cos(inner), np.sin(inner)
    ahead = np.block([[cosine, -sine], [sine, cosine]])
    return (
        first,
        np.cos(twist).astype(np.float32),
        np.sin(twist).astype(np.float32),
        *split_table(ahead),
        *split_table(ahead.T),
        last,
    )


def product(left, right):
    return lax.dot_general(left, right, (((1,), (0,)), ((), ())), preferred_element_type=jnp.float32)


def gather_body(key_ref, value_ref, grad_ref, query_ref, taps_ref, input_ref, sent_ref, features_ref):
    for part in range(8):
        cols = pl.ds(part * 128, 128)
        mixed = key_ref[:, cols].astype(jnp.float32) * value_ref[:, cols].astype(jnp.float32)
        gated = grad_ref[:, cols].astype(jnp.float32) * query_ref[:, cols].astype(jnp.float32)
        for place, signal in enumerate((mixed, taps_ref[:, cols].astype(jnp.float32), gated)):
            turned = signal.T.astype(jnp.bfloat16)
            sent_ref[pl.ds(part * 8, 8), pl.ds(place * 16, 16), :] = turned.reshape(8, 16, 128)
    for near in range(8):
        features_ref[near] = jnp.concatenate(
            [input_ref[:, near * 64 : near * 64 + 64], input_ref[:, 512 + near * 64 : 576 + near * 64]],
            axis=1,
        )


def gather_signals(gate_key, value_proj, grad_out, gate_query, filter_taps, layer_input):
    return pl.pallas_call(
        gather_body,
        out_shape=(
            jax.ShapeDtypeStruct((BLOCKS, LANES, ROWS), jnp.bfloat16),
            jax.ShapeDtypeStruct((8, ROWS, 128), jnp.bfloat16),
        ),
        name="gather_signals",
    )(gate_key, value_proj, grad_out, gate_query, filter_taps, layer_input)


UNROLL = 2


def convolve_body(
    signals_ref, first_ref, cos_ref, sin_ref, ahead_ref, ahead_low_ref, back_ref, back_low_ref, last_ref,
    out_ref, wide_in, wide_out,
):
    wide_in[...] = signals_ref[...].astype(jnp.float32).reshape(BLOCKS * LANES, ROWS)
    first = first_ref[...]
    cosine = cos_ref[...]
    sine = sin_ref[...]

    def channel(place):
        rows = jnp.concatenate(
            [wide_in[pl.ds(place + CHANNELS * s, BLOCKS, stride=LANES), :] for s in range(3)], axis=1
        ).astype(jnp.bfloat16)
        outer = product(first, jnp.concatenate([rows, rows], axis=0))
        turned = []
        for s in range(3):
            real_part = outer[:128, s * 128 : s * 128 + 128]
            other_part = outer[128:, s * 128 : s * 128 + 128]
            turned_real = (real_part * cosine + other_part * sine).astype(jnp.bfloat16)
            turned_other = (other_part * cosine - real_part * sine).astype(jnp.bfloat16)
            turned.append(jnp.concatenate([turned_real, turned_other], axis=1))
        turned = jnp.concatenate(turned, axis=0)
        spectra = product(turned, ahead_ref[...]) + product(turned, ahead_low_ref[...])
        mixed_real, mixed_other = spectra[:128, :128], spectra[:128, 128:]
        taps_real, taps_other = spectra[128:256, :128], spectra[128:256, 128:]
        gated_real, gated_other = spectra[256:, :128], spectra[256:, 128:]
        pairs = jnp.concatenate(
            [
                jnp.concatenate(pair, axis=1)
                for pair in (
                    (
                        mixed_real * taps_real - mixed_other * taps_other,
                        mixed_real * taps_other + mixed_other * taps_real,
                    ),
                    (
                        gated_real * taps_real + gated_other * taps_other,
                        gated_other * taps_real - gated_real * taps_other,
                    ),
                    (
                        gated_real * mixed_real + gated_other * mixed_other,
                        gated_other * mixed_real - gated_real * mixed_other,
                    ),
                )
            ],
            axis=0,
        )
        high = pairs.astype(jnp.bfloat16)
        low = (pairs - high.astype(jnp.float32)).astype(jnp.bfloat16)
        rowed = (
            product(high, back_ref[...]) + product(low, back_ref[...]) + product(high, back_low_ref[...])
        )
        bent = []
        for s in range(3):
            real_part = rowed[s * 128 : s * 128 + 128, :128]
            other_part = rowed[s * 128 : s * 128 + 128, 128:]
            bent_real = (real_part * cosine - other_part * sine).astype(jnp.bfloat16)
            bent_other = (real_part * sine + other_part * cosine).astype(jnp.bfloat16)
            bent.append(jnp.concatenate([bent_real, bent_other], axis=0))
        total = product(last_ref[...], jnp.concatenate(bent, axis=1))
        total = total[:BLOCKS] + total[BLOCKS:]
        for s in range(3):
            factor = LAST_SCALE * (ROOT_SCALE if s == 2 else 1.0)
            wide_out[pl.ds(place + CHANNELS * s, BLOCKS, stride=LANES), :] = (
                total[:, s * 128 : s * 128 + 128] * factor
            )

    def step(index, carry):
        for inside in range(UNROLL):
            channel(index * UNROLL + inside)
        return carry

    lax.fori_loop(0, CHANNELS // UNROLL, step, 0)
    out_ref[...] = wide_out[...].reshape(BLOCKS, LANES, ROWS).astype(jnp.bfloat16)


def convolve(signals, tables):
    return pl.pallas_call(
        convolve_body,
        out_shape=jax.ShapeDtypeStruct((BLOCKS, LANES, ROWS), jnp.bfloat16),
        scratch_shapes=[
            pltpu.VMEM((BLOCKS * LANES, ROWS), jnp.float32),
            pltpu.VMEM((BLOCKS * LANES, ROWS), jnp.float32),
        ],
        name="convolve",
    )(signals, *tables)


def finish_body(back_ref, grad_ref, value_ref, key_ref, query_out, key_out, value_out, filter_out):
    for part in range(8):
        cols = pl.ds(part * 128, 128)

        def turned(place):
            block = back_ref[pl.ds(part * 8, 8), pl.ds(place * 16, 16), :]
            return block.reshape(128, 128).astype(jnp.float32).T

        back = turned(1)
        query_out[:, cols] = (grad_ref[:, cols].astype(jnp.float32) * turned(0)).astype(jnp.bfloat16)
        key_out[:, cols] = (back * value_ref[:, cols].astype(jnp.float32)).astype(jnp.bfloat16)
        value_out[:, cols] = (back * key_ref[:, cols].astype(jnp.float32)).astype(jnp.bfloat16)
        filter_out[:, cols] = turned(2).astype(jnp.bfloat16)


def finish(returned, grad_out, value_proj, gate_key):
    shape = jax.ShapeDtypeStruct(grad_out.shape, jnp.bfloat16)
    return pl.pallas_call(finish_body, out_shape=(shape,) * 4, name="finish")(
        returned, grad_out, value_proj, gate_key
    )


def exchange(array, groups=None):
    return lax.all_to_all(
        array, "seq", split_axis=0, concat_axis=0, tiled=True, axis_index_groups=groups
    )


def shards(layer_input, gate_query, gate_key, value_proj, grad_out, filter_taps):
    tables = [jnp.asarray(table) for table in make_tables()]
    sent, features = gather_signals(
        gate_key, value_proj, grad_out, gate_query, filter_taps, layer_input
    )
    features = exchange(features, NEAR).reshape(8 * ROWS, 128)
    features = lax.all_gather(features, "chan", axis=0)
    results = exchange(convolve(exchange(sent), tables))
    grad_query, grad_key, grad_value, grad_filter = finish(results, grad_out, value_proj, gate_key)
    columns = lax.all_gather(grad_value, "seq", axis=0, tiled=True, axis_index_groups=NEAR)
    partial = jnp.einsum("cpf,pn->cfn", features, columns, preferred_element_type=jnp.float32)
    partial = partial.astype(jnp.bfloat16).reshape(8, 64, partial.shape[-1])
    grad_weight = jnp.sum(exchange(partial, FAR).astype(jnp.float32), axis=0) * ROOT_SCALE
    return (grad_query, grad_key, grad_value, grad_filter, grad_weight)


def solution(mesh):
    placed = P("seq", "chan")
    return jax.shard_map(
        shards,
        mesh=mesh,
        in_specs=(placed,) * 6,
        out_specs=(placed,) * 5,
        check_vma=False,
    )
```

```python
import math

import numpy as np

import jax
import jax.numpy as jnp
from jax import lax
from jax.experimental import pallas as pl
from jax.experimental.pallas import tpu as pltpu
from jax.sharding import PartitionSpec as P


BLOCKS = 64
ROWS = 128
CHANNELS = 16
LANES = 3 * CHANNELS
PERIOD = 2 * BLOCKS * ROWS
LAST_SCALE = 1.0 / PERIOD
ROOT_SCALE = 1.0 / math.sqrt(BLOCKS * ROWS)
SENT = 4 * CHANNELS
PLANES = [[32 * z + i for i in range(32)] for z in range(2)]


def along_x(shift):
    return [(s, s // 8 * 8 + (s // 2 + shift) % 4 * 2 + s % 2) for s in range(64)]


def across(flip):
    pairs = []
    for s in range(64):
        place = (s // 8 % 4 * 2 + s % 2) ^ flip
        pairs.append((s, s // 32 * 32 + place // 2 * 8 + s // 2 % 4 * 2 + place % 2))
    return pairs


def along_z(shift):
    pairs = []
    for flat in range(256):
        s, c = divmod(flat, 4)
        place = (s // 32 * 4 + c + shift) % 8
        pairs.append((flat, (place // 4 * 32 + s % 32) * 4 + place % 4))
    return pairs


def opposite():
    return [(s, (s + 32) % 64) for s in range(64)]


def split_table(table):
    high = table.astype(jnp.bfloat16)
    low = (table - high.astype(np.float64)).astype(jnp.bfloat16)
    return high, low


def make_tables():
    freq = np.arange(2 * BLOCKS)
    block = np.arange(BLOCKS)
    row = np.arange(ROWS)
    outer = 2.0 * math.pi * (freq[:, None] * block[None, :] % (2 * BLOCKS)) / (2 * BLOCKS)
    first = np.concatenate([np.cos(outer), -np.sin(outer)], axis=0)
    first = np.concatenate(split_table(first), axis=1)
    last = np.concatenate([np.cos(outer).T, -np.sin(outer).T], axis=1)
    last = np.concatenate(split_table(last), axis=0)
    twist = 2.0 * math.pi * (freq[:, None] * row[None, :] % PERIOD) / PERIOD
    inner = 2.0 * math.pi * (row[:, None] * row[None, :] % ROWS) / ROWS
    cosine, sine = np.cos(inner), np.sin(inner)
    ahead = np.block([[cosine, -sine], [sine, cosine]])
    return (
        first,
        np.cos(twist).astype(np.float32),
        np.sin(twist).astype(np.float32),
        *split_table(ahead),
        *split_table(ahead.T),
        last,
    )


def product(left, right):
    return lax.dot_general(left, right, (((1,), (0,)), ((), ())), preferred_element_type=jnp.float32)


def gather_body(key_ref, value_ref, grad_ref, query_ref, taps_ref, sent_ref):
    for part in range(8):
        cols = pl.ds(part * 128, 128)
        key = key_ref[:, cols].astype(jnp.float32)
        mixed = key * value_ref[:, cols].astype(jnp.float32)
        gated = grad_ref[:, cols].astype(jnp.float32) * query_ref[:, cols].astype(jnp.float32)
        for place, signal in enumerate((mixed, taps_ref[:, cols].astype(jnp.float32), gated, key)):
            turned = signal.T.astype(jnp.bfloat16)
            sent_ref[pl.ds(part * 8, 8), pl.ds(place * 16, 16), :] = turned.reshape(8, 16, 128)


def gather_signals(gate_key, value_proj, grad_out, gate_query, filter_taps):
    return pl.pallas_call(
        gather_body,
        out_shape=jax.ShapeDtypeStruct((BLOCKS, SENT, ROWS), jnp.bfloat16),
        name="gather_signals",
    )(gate_key, value_proj, grad_out, gate_query, filter_taps)


def features_body(where_ref, input_ref, *outs):
    for shift, out_ref in enumerate(outs):
        start = (where_ref[0] + shift) % 4 * 128
        for side in range(2):
            block = input_ref[:, pl.ds(pl.multiple_of(side * 512 + start, 128), 128)]
            out_ref[side * 128 : side * 128 + 128, :] = block.astype(jnp.float32).T.astype(jnp.bfloat16)


def split_features(where, layer_input):
    return pl.pallas_call(
        features_body,
        out_shape=(jax.ShapeDtypeStruct((256, ROWS), jnp.bfloat16),) * 4,
        in_specs=[
            pl.BlockSpec(memory_space=pltpu.SMEM),
            pl.BlockSpec(memory_space=pltpu.VMEM),
        ],
        name="split_features",
    )(where, layer_input)


UNROLL = 2


def convolve_body(
    signals_ref, first_ref, cos_ref, sin_ref, ahead_ref, ahead_low_ref, back_ref, back_low_ref, last_ref,
    out_ref, value_ref, wide_in, wide_out, wide_value,
):
    wide_in[...] = signals_ref[...].astype(jnp.float32).reshape(BLOCKS * SENT, ROWS)
    first = first_ref[...]
    cosine = cos_ref[...]
    sine = sin_ref[...]

    def channel(place):
        rows = jnp.concatenate(
            [wide_in[pl.ds(place + CHANNELS * s, BLOCKS, stride=SENT), :] for s in range(3)], axis=1
        ).astype(jnp.bfloat16)
        outer = product(first, jnp.concatenate([rows, rows], axis=0))
        turned = []
        for s in range(3):
            real_part = outer[:128, s * 128 : s * 128 + 128]
            other_part = outer[128:, s * 128 : s * 128 + 128]
            turned_real = (real_part * cosine + other_part * sine).astype(jnp.bfloat16)
            turned_other = (other_part * cosine - real_part * sine).astype(jnp.bfloat16)
            turned.append(jnp.concatenate([turned_real, turned_other], axis=1))
        turned = jnp.concatenate(turned, axis=0)
        spectra = product(turned, ahead_ref[...]) + product(turned, ahead_low_ref[...])
        mixed_real, mixed_other = spectra[:128, :128], spectra[:128, 128:]
        taps_real, taps_other = spectra[128:256, :128], spectra[128:256, 128:]
        gated_real, gated_other = spectra[256:, :128], spectra[256:, 128:]
        pairs = jnp.concatenate(
            [
                jnp.concatenate(pair, axis=1)
                for pair in (
                    (
                        mixed_real * taps_real - mixed_other * taps_other,
                        mixed_real * taps_other + mixed_other * taps_real,
                    ),
                    (
                        gated_real * taps_real + gated_other * taps_other,
                        gated_other * taps_real - gated_real * taps_other,
                    ),
                    (
                        gated_real * mixed_real + gated_other * mixed_other,
                        gated_other * mixed_real - gated_real * mixed_other,
                    ),
                )
            ],
            axis=0,
        )
        high = pairs.astype(jnp.bfloat16)
        low = (pairs - high.astype(jnp.float32)).astype(jnp.bfloat16)
        rowed = (
            product(high, back_ref[...]) + product(low, back_ref[...]) + product(high, back_low_ref[...])
        )
        bent = []
        for s in range(3):
            real_part = rowed[s * 128 : s * 128 + 128, :128]
            other_part = rowed[s * 128 : s * 128 + 128, 128:]
            bent_real = (real_part * cosine - other_part * sine).astype(jnp.bfloat16)
            bent_other = (real_part * sine + other_part * cosine).astype(jnp.bfloat16)
            bent.append(jnp.concatenate([bent_real, bent_other], axis=0))
        total = product(last_ref[...], jnp.concatenate(bent, axis=1))
        total = total[:BLOCKS] + total[BLOCKS:]
        for s in range(3):
            factor = LAST_SCALE * (ROOT_SCALE if s == 2 else 1.0)
            wide_out[pl.ds(place + CHANNELS * s, BLOCKS, stride=LANES), :] = (
                total[:, s * 128 : s * 128 + 128] * factor
            )
        back = (total[:, 128:256] * LAST_SCALE).astype(jnp.bfloat16).astype(jnp.float32)
        key = wide_in[pl.ds(place + CHANNELS * 3, BLOCKS, stride=SENT), :]
        wide_value[pl.ds(place, BLOCKS, stride=CHANNELS), :] = back * key

    def step(index, carry):
        for inside in range(UNROLL):
            channel(index * UNROLL + inside)
        return carry

    lax.fori_loop(0, CHANNELS // UNROLL, step, 0)
    out_ref[...] = wide_out[...].reshape(BLOCKS, LANES, ROWS).astype(jnp.bfloat16)
    for block in range(BLOCKS):
        tile = wide_value[block * CHANNELS : block * CHANNELS + CHANNELS, :].astype(jnp.bfloat16)
        z, y, x, core = block // 32, block // 8 % 4, block // 2 % 4, block % 2
        for target in range(4):
            value_ref[y * 8 + target * 2 + core, z * 4 + x] = tile


def convolve(signals, tables):
    return pl.pallas_call(
        convolve_body,
        out_shape=(
            jax.ShapeDtypeStruct((BLOCKS, LANES, ROWS), jnp.bfloat16),
            jax.ShapeDtypeStruct((32, 8, CHANNELS, ROWS), jnp.bfloat16),
        ),
        scratch_shapes=[
            pltpu.VMEM((BLOCKS * SENT, ROWS), jnp.float32),
            pltpu.VMEM((BLOCKS * LANES, ROWS), jnp.float32),
            pltpu.VMEM((BLOCKS * CHANNELS, ROWS), jnp.float32),
        ],
        name="convolve",
    )(signals, *tables)


def finish_body(back_ref, grad_ref, value_ref, key_ref, query_out, key_out, value_out, filter_out):
    for part in range(8):
        cols = pl.ds(part * 128, 128)

        def turned(place):
            block = back_ref[pl.ds(part * 8, 8), pl.ds(place * 16, 16), :]
            return block.reshape(128, 128).astype(jnp.float32).T

        back = turned(1)
        query_out[:, cols] = (grad_ref[:, cols].astype(jnp.float32) * turned(0)).astype(jnp.bfloat16)
        key_out[:, cols] = (back * value_ref[:, cols].astype(jnp.float32)).astype(jnp.bfloat16)
        value_out[:, cols] = (back * key_ref[:, cols].astype(jnp.float32)).astype(jnp.bfloat16)
        filter_out[:, cols] = turned(2).astype(jnp.bfloat16)


def finish(returned, grad_out, value_proj, gate_key):
    shape = jax.ShapeDtypeStruct(grad_out.shape, jnp.bfloat16)
    return pl.pallas_call(finish_body, out_shape=(shape,) * 4, name="finish")(
        returned, grad_out, value_proj, gate_key
    )


def weight_body(where_ref, value_ref, *refs):
    features, outs, (aligned, pieces) = refs[:8], refs[8:16], refs[16:]
    x, ring, place = where_ref[0], where_ref[1], where_ref[2]
    for z in range(2):
        for back in range(4):
            block = value_ref[:, z * 4 + (x - back + 4) % 4]
            aligned[z, :, back * 128 : back * 128 + 128] = block.reshape(512, ROWS)
    for apart in range(4):
        total = None
        for half in range(2):
            source = (ring - apart - 4 * half + 8) % 8
            rows = features[apart + 4 * half]
            rows = jnp.concatenate([rows[back] for back in range(4)], axis=1)
            term = lax.dot_general(
                rows, aligned[source // 4], (((1,), (1,)), ((), ())), preferred_element_type=jnp.float32
            )
            total = term if total is None else total + term
        group = (ring - apart + 8) % 4
        for side in range(2):
            for core in range(2):
                target = ((group % 2) * 2 + side) * 2 + core
                start = side * 128 + core * 64
                pieces[target * 2 + group // 2] = total[start : start + 64].astype(jnp.bfloat16)
    for flip, out_ref in enumerate(outs):
        out_ref[...] = pieces[pl.ds((place ^ flip) * 2, 2)]


def weight_parts(where, value, features):
    return pl.pallas_call(
        weight_body,
        out_shape=(jax.ShapeDtypeStruct((2, 64, 512), jnp.bfloat16),) * 8,
        in_specs=[pl.BlockSpec(memory_space=pltpu.SMEM)] + [pl.BlockSpec(memory_space=pltpu.VMEM)] * 9,
        scratch_shapes=[
            pltpu.VMEM((2, 512, 512), jnp.bfloat16),
            pltpu.VMEM((16, 64, 512), jnp.bfloat16),
        ],
        name="weight_parts",
    )(where, value, *features)


def total_body(where_ref, *refs):
    parts, (kept_ref, sent_ref) = refs[:8], refs[8:]
    z = where_ref[3]
    for out_ref, place in ((kept_ref, z), (sent_ref, 1 - z)):
        total = parts[0][place].astype(jnp.float32)
        for part in parts[1:]:
            total = total + part[place].astype(jnp.float32)
        out_ref[...] = total * ROOT_SCALE


def weight_total(where, parts):
    return pl.pallas_call(
        total_body,
        out_shape=(jax.ShapeDtypeStruct((64, 512), jnp.float32),) * 2,
        in_specs=[pl.BlockSpec(memory_space=pltpu.SMEM)] + [pl.BlockSpec(memory_space=pltpu.VMEM)] * 8,
        name="weight_total",
    )(where, *parts)


def exchange(array, groups=None):
    return lax.all_to_all(
        array, "seq", split_axis=0, concat_axis=0, tiled=True, axis_index_groups=groups
    )


def ring_step(array, shift):
    return lax.ppermute(array, ("seq", "chan"), along_z(shift))


def shards(layer_input, gate_query, gate_key, value_proj, grad_out, filter_taps):
    tables = [jnp.asarray(table) for table in make_tables()]
    index = lax.axis_index("seq")
    z, y, x, core = index // 32, index // 8 % 4, index // 2 % 4, index % 2
    where = jnp.stack([x, z * 4 + lax.axis_index("chan"), y * 2 + core, z]).astype(jnp.int32)
    pieces = split_features(where, layer_input)
    own = [lax.ppermute(pieces[n], "seq", along_x(n)) for n in range(1, 4)]
    own = jnp.stack([pieces[0]] + own)
    sent = gather_signals(gate_key, value_proj, grad_out, gate_query, filter_taps)
    up, down = ring_step(own, 1), ring_step(own, -1)
    signals = exchange(sent)
    up2, down2 = ring_step(up, 1), ring_step(down, -1)
    results, value = convolve(signals, tables)
    up3, down3, far = ring_step(up2, 1), ring_step(down2, -1), ring_step(up2, 2)
    value = exchange(value, PLANES)
    parts = weight_parts(where, value, (own, up, up2, up3, far, down3, down2, down))
    parts = [parts[0]] + [lax.ppermute(parts[n], "seq", across(n)) for n in range(1, 8)]
    results = exchange(results)
    kept, sent = weight_total(where, parts)
    received = lax.ppermute(sent, "seq", opposite())
    grad_query, grad_key, grad_value, grad_filter = finish(
        results, grad_out, value_proj, gate_key
    )
    grad_weight = jnp.where(
        z == 0,
        jnp.concatenate([kept, received], axis=1),
        jnp.concatenate([received, kept], axis=1),
    )
    return (grad_query, grad_key, grad_value, grad_filter, grad_weight)


def solution(mesh):
    placed = P("seq", "chan")
    return jax.shard_map(
        shards,
        mesh=mesh,
        in_specs=(placed,) * 6,
        out_specs=(placed,) * 5,
        check_vma=False,
    )
```

```python
import math

import numpy as np

import jax
import jax.numpy as jnp
from jax import lax
from jax.experimental import pallas as pl
from jax.experimental.pallas import tpu as pltpu
from jax.sharding import PartitionSpec as P


BLOCKS = 64
ROWS = 128
CHANNELS = 16
LANES = 3 * CHANNELS
PERIOD = 2 * BLOCKS * ROWS
LAST_SCALE = 1.0 / PERIOD
KEPT = 72
ROOT_SCALE = 1.0 / math.sqrt(BLOCKS * ROWS)
SENT = 4 * CHANNELS
PLANES = [[32 * z + i for i in range(32)] for z in range(2)]


def along_x(shift):
    return [(s, s // 8 * 8 + (s // 2 + shift) % 4 * 2 + s % 2) for s in range(64)]


def across(flip):
    pairs = []
    for s in range(64):
        place = (s // 8 % 4 * 2 + s % 2) ^ flip
        pairs.append((s, s // 32 * 32 + place // 2 * 8 + s // 2 % 4 * 2 + place % 2))
    return pairs


def along_z(shift):
    pairs = []
    for flat in range(256):
        s, c = divmod(flat, 4)
        place = (s // 32 * 4 + c + shift) % 8
        pairs.append((flat, (place // 4 * 32 + s % 32) * 4 + place % 4))
    return pairs


def opposite():
    return [(s, (s + 32) % 64) for s in range(64)]


def split_table(table):
    high = table.astype(jnp.bfloat16)
    low = (table - high.astype(np.float64)).astype(jnp.bfloat16)
    return high, low


def make_tables():
    freq = np.arange(KEPT)
    block = np.arange(BLOCKS)
    row = np.arange(ROWS)
    outer = 2.0 * math.pi * (freq[:, None] * block[None, :] % (2 * BLOCKS)) / (2 * BLOCKS)
    first = np.concatenate([np.cos(outer), -np.sin(outer)], axis=0)
    first = np.concatenate(split_table(first), axis=1)
    weight = np.where((freq == 0) | (freq == BLOCKS), 1.0, np.where(freq < BLOCKS, 2.0, 0.0))
    last = np.concatenate([np.cos(outer).T * weight, -np.sin(outer).T * weight], axis=1)
    last = np.concatenate(split_table(last), axis=0)
    twist = 2.0 * math.pi * (freq[:, None] * row[None, :] % PERIOD) / PERIOD
    inner = 2.0 * math.pi * (row[:, None] * row[None, :] % ROWS) / ROWS
    cosine, sine = np.cos(inner), np.sin(inner)
    ahead = np.block([[cosine, -sine], [sine, cosine]])
    back_high, back_low = split_table(ahead.T)
    return (
        first,
        np.cos(twist).astype(np.float32),
        np.sin(twist).astype(np.float32),
        np.concatenate(split_table(ahead), axis=0),
        np.concatenate([back_high, back_high, back_low], axis=0),
        last,
    )


def product(left, right):
    return lax.dot_general(left, right, (((1,), (0,)), ((), ())), preferred_element_type=jnp.float32)


def gather_body(key_ref, value_ref, grad_ref, query_ref, taps_ref, sent_ref):
    for part in range(8):
        cols = pl.ds(part * 128, 128)
        key = key_ref[:, cols].astype(jnp.float32)
        mixed = key * value_ref[:, cols].astype(jnp.float32)
        gated = grad_ref[:, cols].astype(jnp.float32) * query_ref[:, cols].astype(jnp.float32)
        for place, signal in enumerate((mixed, taps_ref[:, cols].astype(jnp.float32), gated, key)):
            turned = signal.T.astype(jnp.bfloat16)
            sent_ref[pl.ds(part * 8, 8), pl.ds(place * 16, 16), :] = turned.reshape(8, 16, 128)


def gather_signals(gate_key, value_proj, grad_out, gate_query, filter_taps):
    return pl.pallas_call(
        gather_body,
        out_shape=jax.ShapeDtypeStruct((BLOCKS, SENT, ROWS), jnp.bfloat16),
        name="gather_signals",
    )(gate_key, value_proj, grad_out, gate_query, filter_taps)


def features_body(where_ref, input_ref, *outs):
    for shift, out_ref in enumerate(outs):
        start = (where_ref[0] + shift) % 4 * 128
        for side in range(2):
            block = input_ref[:, pl.ds(pl.multiple_of(side * 512 + start, 128), 128)]
            out_ref[side * 128 : side * 128 + 128, :] = block.astype(jnp.float32).T.astype(jnp.bfloat16)


def split_features(where, layer_input):
    return pl.pallas_call(
        features_body,
        out_shape=(jax.ShapeDtypeStruct((256, ROWS), jnp.bfloat16),) * 4,
        in_specs=[
            pl.BlockSpec(memory_space=pltpu.SMEM),
            pl.BlockSpec(memory_space=pltpu.VMEM),
        ],
        name="split_features",
    )(where, layer_input)


UNROLL = 2


def convolve_body(
    signals_ref, first_ref, cos_ref, sin_ref, ahead_ref, back_ref, last_ref,
    out_ref, value_ref, wide_in, wide_out, wide_value,
):
    wide_in[...] = signals_ref[...].astype(jnp.float32).reshape(BLOCKS * SENT, ROWS)

    def step(index, carry):
        cosine = cos_ref[...]
        sine = sin_ref[...]
        places = [index * UNROLL + inside for inside in range(UNROLL)]
        number = 3 * UNROLL
        rows = jnp.concatenate(
            [
                wide_in[pl.ds(place + CHANNELS * s, BLOCKS, stride=SENT), :]
                for place in places
                for s in range(3)
            ],
            axis=1,
        ).astype(jnp.bfloat16)
        outer = product(first_ref[...], jnp.concatenate([rows, rows], axis=0))
        turned = []
        for n in range(number):
            real_part = outer[:KEPT, n * 128 : n * 128 + 128]
            other_part = outer[KEPT:, n * 128 : n * 128 + 128]
            turned.append(
                jnp.concatenate(
                    [
                        real_part * cosine + other_part * sine,
                        other_part * cosine - real_part * sine,
                    ],
                    axis=1,
                )
            )
        turned = jnp.concatenate(turned, axis=0).astype(jnp.bfloat16)
        spectra = product(jnp.concatenate([turned, turned], axis=1), ahead_ref[...])
        pairs = []
        for n in range(UNROLL):
            parts = [
                (spectra[start : start + KEPT, :128], spectra[start : start + KEPT, 128:])
                for start in range(3 * n * KEPT, (3 * n + 3) * KEPT, KEPT)
            ]
            (mixed_real, mixed_other), (taps_real, taps_other), (gated_real, gated_other) = parts
            for pair in (
                (
                    mixed_real * taps_real - mixed_other * taps_other,
                    mixed_real * taps_other + mixed_other * taps_real,
                ),
                (
                    gated_real * taps_real + gated_other * taps_other,
                    gated_other * taps_real - gated_real * taps_other,
                ),
                (
                    gated_real * mixed_real + gated_other * mixed_other,
                    gated_other * mixed_real - gated_real * mixed_other,
                ),
            ):
                pairs.append(jnp.concatenate(pair, axis=1))
        pairs = jnp.concatenate(pairs, axis=0)
        high = pairs.astype(jnp.bfloat16)
        low = (pairs - high.astype(jnp.float32)).astype(jnp.bfloat16)
        rowed = product(jnp.concatenate([high, low, high], axis=1), back_ref[...])
        bent = []
        for n in range(number):
            real_part = rowed[n * KEPT : n * KEPT + KEPT, :128]
            other_part = rowed[n * KEPT : n * KEPT + KEPT, 128:]
            bent.append(
                jnp.concatenate(
                    [
                        real_part * cosine - other_part * sine,
                        real_part * sine + other_part * cosine,
                    ],
                    axis=0,
                )
            )
        total = product(last_ref[...], jnp.concatenate(bent, axis=1).astype(jnp.bfloat16))
        total = total[:BLOCKS] + total[BLOCKS:]
        for n in range(number):
            s, place = n % 3, places[n // 3]
            factor = LAST_SCALE * (ROOT_SCALE if s == 2 else 1.0)
            result = total[:, n * 128 : n * 128 + 128] * factor
            wide_out[pl.ds(place + CHANNELS * s, BLOCKS, stride=LANES), :] = result
            if s == 1:
                key = wide_in[pl.ds(place + CHANNELS * 3, BLOCKS, stride=SENT), :]
                wide_value[pl.ds(place, BLOCKS, stride=CHANNELS), :] = (
                    result.astype(jnp.bfloat16).astype(jnp.float32) * key
                )
        return carry

    lax.fori_loop(0, CHANNELS // UNROLL, step, 0)
    out_ref[...] = wide_out[...].reshape(BLOCKS, LANES, ROWS).astype(jnp.bfloat16)
    for block in range(BLOCKS):
        tile = wide_value[block * CHANNELS : block * CHANNELS + CHANNELS, :].astype(jnp.bfloat16)
        z, y, x, core = block // 32, block // 8 % 4, block // 2 % 4, block % 2
        for target in range(4):
            value_ref[y * 8 + target * 2 + core, z * 4 + x] = tile


def convolve(signals, tables):
    return pl.pallas_call(
        convolve_body,
        out_shape=(
            jax.ShapeDtypeStruct((BLOCKS, LANES, ROWS), jnp.bfloat16),
            jax.ShapeDtypeStruct((32, 8, CHANNELS, ROWS), jnp.bfloat16),
        ),
        scratch_shapes=[
            pltpu.VMEM((BLOCKS * SENT, ROWS), jnp.float32),
            pltpu.VMEM((BLOCKS * LANES, ROWS), jnp.float32),
            pltpu.VMEM((BLOCKS * CHANNELS, ROWS), jnp.float32),
        ],
        name="convolve",
    )(signals, *tables)


def finish_body(back_ref, grad_ref, value_ref, key_ref, query_out, key_out, value_out, filter_out):
    for part in range(8):
        cols = pl.ds(part * 128, 128)

        def turned(place):
            block = back_ref[pl.ds(part * 8, 8), pl.ds(place * 16, 16), :]
            return block.reshape(128, 128).astype(jnp.float32).T

        back = turned(1)
        query_out[:, cols] = (grad_ref[:, cols].astype(jnp.float32) * turned(0)).astype(jnp.bfloat16)
        key_out[:, cols] = (back * value_ref[:, cols].astype(jnp.float32)).astype(jnp.bfloat16)
        value_out[:, cols] = (back * key_ref[:, cols].astype(jnp.float32)).astype(jnp.bfloat16)
        filter_out[:, cols] = turned(2).astype(jnp.bfloat16)


def finish(returned, grad_out, value_proj, gate_key):
    shape = jax.ShapeDtypeStruct(grad_out.shape, jnp.bfloat16)
    return pl.pallas_call(finish_body, out_shape=(shape,) * 4, name="finish")(
        returned, grad_out, value_proj, gate_key
    )


def weight_body(where_ref, value_ref, *refs):
    features, outs, (aligned, pieces) = refs[:8], refs[8:16], refs[16:]
    x, ring, place = where_ref[0], where_ref[1], where_ref[2]
    for z in range(2):
        for back in range(4):
            block = value_ref[:, z * 4 + (x - back + 4) % 4]
            aligned[z, :, back * 128 : back * 128 + 128] = block.reshape(512, ROWS)
    for apart in range(4):
        total = None
        for half in range(2):
            source = (ring - apart - 4 * half + 8) % 8
            rows = features[apart + 4 * half]
            rows = jnp.concatenate([rows[back] for back in range(4)], axis=1)
            term = lax.dot_general(
                rows, aligned[source // 4], (((1,), (1,)), ((), ())), preferred_element_type=jnp.float32
            )
            total = term if total is None else total + term
        group = (ring - apart + 8) % 4
        for side in range(2):
            for core in range(2):
                target = ((group % 2) * 2 + side) * 2 + core
                start = side * 128 + core * 64
                pieces[target * 2 + group // 2] = total[start : start + 64].astype(jnp.bfloat16)
    for flip, out_ref in enumerate(outs):
        out_ref[...] = pieces[pl.ds((place ^ flip) * 2, 2)]


def weight_parts(where, value, features):
    return pl.pallas_call(
        weight_body,
        out_shape=(jax.ShapeDtypeStruct((2, 64, 512), jnp.bfloat16),) * 8,
        in_specs=[pl.BlockSpec(memory_space=pltpu.SMEM)] + [pl.BlockSpec(memory_space=pltpu.VMEM)] * 9,
        scratch_shapes=[
            pltpu.VMEM((2, 512, 512), jnp.bfloat16),
            pltpu.VMEM((16, 64, 512), jnp.bfloat16),
        ],
        name="weight_parts",
    )(where, value, *features)


def total_body(where_ref, *refs):
    parts, (kept_ref, sent_ref) = refs[:8], refs[8:]
    z = where_ref[3]
    for out_ref, place in ((kept_ref, z), (sent_ref, 1 - z)):
        total = parts[0][place].astype(jnp.float32)
        for part in parts[1:]:
            total = total + part[place].astype(jnp.float32)
        out_ref[...] = total * ROOT_SCALE


def weight_total(where, parts):
    return pl.pallas_call(
        total_body,
        out_shape=(jax.ShapeDtypeStruct((64, 512), jnp.float32),) * 2,
        in_specs=[pl.BlockSpec(memory_space=pltpu.SMEM)] + [pl.BlockSpec(memory_space=pltpu.VMEM)] * 8,
        name="weight_total",
    )(where, *parts)


def exchange(array, groups=None):
    return lax.all_to_all(
        array, "seq", split_axis=0, concat_axis=0, tiled=True, axis_index_groups=groups
    )


def ring_step(array, shift):
    return lax.ppermute(array, ("seq", "chan"), along_z(shift))


def shards(layer_input, gate_query, gate_key, value_proj, grad_out, filter_taps):
    tables = [jnp.asarray(table) for table in make_tables()]
    index = lax.axis_index("seq")
    z, y, x, core = index // 32, index // 8 % 4, index // 2 % 4, index % 2
    where = jnp.stack([x, z * 4 + lax.axis_index("chan"), y * 2 + core, z]).astype(jnp.int32)
    pieces = split_features(where, layer_input)
    own = [lax.ppermute(pieces[n], "seq", along_x(n)) for n in range(1, 4)]
    own = jnp.stack([pieces[0]] + own)
    sent = gather_signals(gate_key, value_proj, grad_out, gate_query, filter_taps)
    up, down = ring_step(own, 1), ring_step(own, -1)
    signals = exchange(sent)
    up2, down2 = ring_step(up, 1), ring_step(down, -1)
    results, value = convolve(signals, tables)
    up3, down3, far = ring_step(up2, 1), ring_step(down2, -1), ring_step(up2, 2)
    value = exchange(value, PLANES)
    parts = weight_parts(where, value, (own, up, up2, up3, far, down3, down2, down))
    parts = [parts[0]] + [lax.ppermute(parts[n], "seq", across(n)) for n in range(1, 8)]
    results = exchange(results)
    kept, sent = weight_total(where, parts)
    received = lax.ppermute(sent, "seq", opposite())
    grad_query, grad_key, grad_value, grad_filter = finish(results, grad_out, value_proj, gate_key)
    grad_weight = jnp.where(
        z == 0,
        jnp.concatenate([kept, received], axis=1),
        jnp.concatenate([received, kept], axis=1),
    )
    return (grad_query, grad_key, grad_value, grad_filter, grad_weight)


def solution(mesh):
    placed = P("seq", "chan")
    return jax.shard_map(
        shards,
        mesh=mesh,
        in_specs=(placed,) * 6,
        out_specs=(placed,) * 5,
        check_vma=False,
    )
```

```python
import math

import numpy as np

import jax
import jax.numpy as jnp
from jax import lax
from jax.experimental import pallas as pl
from jax.experimental.pallas import tpu as pltpu
from jax.sharding import PartitionSpec as P


BLOCKS = 64
ROWS = 128
CHANNELS = 16
LANES = 3 * CHANNELS
PERIOD = 2 * BLOCKS * ROWS
LAST_SCALE = 1.0 / PERIOD
KEPT = 72
VMEM_GRANT = 12 << 20
ROOT_SCALE = 1.0 / math.sqrt(BLOCKS * ROWS)
SENT = 4 * CHANNELS
PLANES = [[32 * z + i for i in range(32)] for z in range(2)]


def along_x(shift):
    return [(s, s // 8 * 8 + (s // 2 + shift) % 4 * 2 + s % 2) for s in range(64)]


def across(flip):
    pairs = []
    for s in range(64):
        place = (s // 8 % 4 * 2 + s % 2) ^ flip
        pairs.append((s, s // 32 * 32 + place // 2 * 8 + s // 2 % 4 * 2 + place % 2))
    return pairs


def along_z(shift):
    pairs = []
    for flat in range(256):
        s, c = divmod(flat, 4)
        place = (s // 32 * 4 + c + shift) % 8
        pairs.append((flat, (place // 4 * 32 + s % 32) * 4 + place % 4))
    return pairs


def opposite():
    return [(s, (s + 32) % 64) for s in range(64)]


def split_table(table):
    high = table.astype(jnp.bfloat16)
    low = (table - high.astype(np.float64)).astype(jnp.bfloat16)
    return high, low


def make_tables():
    freq = np.arange(KEPT)
    block = np.arange(BLOCKS)
    row = np.arange(ROWS)
    outer = 2.0 * math.pi * (freq[:, None] * block[None, :] % (2 * BLOCKS)) / (2 * BLOCKS)
    first = np.concatenate([np.cos(outer), -np.sin(outer)], axis=0)
    first = np.concatenate(split_table(first), axis=1)
    weight = np.where((freq == 0) | (freq == BLOCKS), 1.0, np.where(freq < BLOCKS, 2.0, 0.0))
    last = np.concatenate([np.cos(outer).T * weight, -np.sin(outer).T * weight], axis=1)
    last = np.concatenate(split_table(last), axis=0)
    twist = 2.0 * math.pi * (freq[:, None] * row[None, :] % PERIOD) / PERIOD
    inner = 2.0 * math.pi * (row[:, None] * row[None, :] % ROWS) / ROWS
    cosine, sine = np.cos(inner), np.sin(inner)
    ahead = np.block([[cosine, -sine], [sine, cosine]])
    return (
        first,
        np.cos(twist).astype(np.float32),
        np.sin(twist).astype(np.float32),
        np.concatenate(split_table(ahead), axis=0),
        np.concatenate(split_table(ahead.T), axis=0),
        last,
    )


def product(left, right):
    return lax.dot_general(left, right, (((1,), (0,)), ((), ())), preferred_element_type=jnp.float32)


def gather_body(key_ref, value_ref, grad_ref, query_ref, taps_ref, sent_ref):
    for part in range(8):
        cols = pl.ds(part * 128, 128)
        key = key_ref[:, cols].astype(jnp.float32)
        mixed = key * value_ref[:, cols].astype(jnp.float32)
        gated = grad_ref[:, cols].astype(jnp.float32) * query_ref[:, cols].astype(jnp.float32)
        for place, signal in enumerate((mixed, taps_ref[:, cols].astype(jnp.float32), gated, key)):
            turned = signal.T.astype(jnp.bfloat16)
            sent_ref[pl.ds(part * 8, 8), pl.ds(place * 16, 16), :] = turned.reshape(8, 16, 128)


def gather_signals(gate_key, value_proj, grad_out, gate_query, filter_taps):
    return pl.pallas_call(
        gather_body,
        out_shape=jax.ShapeDtypeStruct((BLOCKS, SENT, ROWS), jnp.bfloat16),
        name="gather_signals",
        compiler_params=pltpu.CompilerParams(vmem_limit_bytes=VMEM_GRANT),
    )(gate_key, value_proj, grad_out, gate_query, filter_taps)


def features_body(where_ref, input_ref, *outs):
    for shift, out_ref in enumerate(outs):
        start = (where_ref[0] + shift) % 4 * 128
        for side in range(2):
            block = input_ref[:, pl.ds(pl.multiple_of(side * 512 + start, 128), 128)]
            out_ref[side * 128 : side * 128 + 128, :] = block.astype(jnp.float32).T.astype(jnp.bfloat16)


def split_features(where, layer_input):
    return pl.pallas_call(
        features_body,
        out_shape=(jax.ShapeDtypeStruct((256, ROWS), jnp.bfloat16),) * 4,
        in_specs=[
            pl.BlockSpec(memory_space=pltpu.SMEM),
            pl.BlockSpec(memory_space=pltpu.VMEM),
        ],
        name="split_features",
        compiler_params=pltpu.CompilerParams(vmem_limit_bytes=VMEM_GRANT),
    )(where, layer_input)


UNROLL = 4


def invert(pairs, number, cosine, sine, back_ref, last_ref):
    rowed = product(jnp.concatenate([pairs, pairs], axis=1), back_ref[...])
    bent = []
    for n in range(number):
        real_part = rowed[n * KEPT : n * KEPT + KEPT, :128]
        other_part = rowed[n * KEPT : n * KEPT + KEPT, 128:]
        bent.append(
            jnp.concatenate(
                [
                    real_part * cosine - other_part * sine,
                    real_part * sine + other_part * cosine,
                ],
                axis=0,
            )
        )
    total = product(last_ref[...], jnp.concatenate(bent, axis=1).astype(jnp.bfloat16))
    return total[:BLOCKS] + total[BLOCKS:]


def convolve_body(
    signals_ref, first_ref, cos_ref, sin_ref, ahead_ref, back_ref, last_ref,
    out_ref, value_ref, rest_ref, wide_in, wide_out, wide_value,
):
    wide_in[...] = signals_ref[...].astype(jnp.float32).reshape(BLOCKS * SENT, ROWS)

    def step(index, carry):
        cosine = cos_ref[...]
        sine = sin_ref[...]
        places = [index * UNROLL + inside for inside in range(UNROLL)]
        rows = jnp.concatenate(
            [
                wide_in[pl.ds(place + CHANNELS * s, BLOCKS, stride=SENT), :]
                for place in places
                for s in range(3)
            ],
            axis=1,
        ).astype(jnp.bfloat16)
        outer = product(first_ref[...], jnp.concatenate([rows, rows], axis=0))
        turned = []
        for n in range(3 * UNROLL):
            real_part = outer[:KEPT, n * 128 : n * 128 + 128]
            other_part = outer[KEPT:, n * 128 : n * 128 + 128]
            turned.append(
                jnp.concatenate(
                    [
                        real_part * cosine + other_part * sine,
                        other_part * cosine - real_part * sine,
                    ],
                    axis=1,
                )
            )
        turned = jnp.concatenate(turned, axis=0).astype(jnp.bfloat16)
        spectra = product(jnp.concatenate([turned, turned], axis=1), ahead_ref[...])
        firsts, rest = [], []
        for n in range(UNROLL):
            parts = [
                (spectra[start : start + KEPT, :128], spectra[start : start + KEPT, 128:])
                for start in range(3 * n * KEPT, (3 * n + 3) * KEPT, KEPT)
            ]
            (mixed_real, mixed_other), (taps_real, taps_other), (gated_real, gated_other) = parts
            firsts.append(
                jnp.concatenate(
                    [
                        gated_real * taps_real + gated_other * taps_other,
                        gated_other * taps_real - gated_real * taps_other,
                    ],
                    axis=1,
                )
            )
            rest.append(
                jnp.concatenate(
                    [
                        mixed_real * taps_real - mixed_other * taps_other,
                        mixed_real * taps_other + mixed_other * taps_real,
                    ],
                    axis=1,
                )
            )
            rest.append(
                jnp.concatenate(
                    [
                        gated_real * mixed_real + gated_other * mixed_other,
                        gated_other * mixed_real - gated_real * mixed_other,
                    ],
                    axis=1,
                )
            )
        rest_ref[index] = jnp.concatenate(rest, axis=0).astype(jnp.bfloat16)
        firsts = jnp.concatenate(firsts, axis=0).astype(jnp.bfloat16)
        total = invert(firsts, UNROLL, cosine, sine, back_ref, last_ref)
        for n, place in enumerate(places):
            result = total[:, n * 128 : n * 128 + 128] * LAST_SCALE
            wide_out[pl.ds(place, BLOCKS, stride=CHANNELS), :] = result
            key = wide_in[pl.ds(place + CHANNELS * 3, BLOCKS, stride=SENT), :]
            wide_value[pl.ds(place, BLOCKS, stride=CHANNELS), :] = (
                result.astype(jnp.bfloat16).astype(jnp.float32) * key
            )
        return carry

    lax.fori_loop(0, CHANNELS // UNROLL, step, 0)
    out_ref[...] = wide_out[...].reshape(BLOCKS, CHANNELS, ROWS).astype(jnp.bfloat16)
    for block in range(BLOCKS):
        tile = wide_value[block * CHANNELS : block * CHANNELS + CHANNELS, :].astype(jnp.bfloat16)
        z, y, x, core = block // 32, block // 8 % 4, block // 2 % 4, block % 2
        for target in range(4):
            value_ref[y * 8 + target * 2 + core, z * 4 + x] = tile


def convolve(signals, tables):
    return pl.pallas_call(
        convolve_body,
        out_shape=(
            jax.ShapeDtypeStruct((BLOCKS, CHANNELS, ROWS), jnp.bfloat16),
            jax.ShapeDtypeStruct((32, 8, CHANNELS, ROWS), jnp.bfloat16),
            jax.ShapeDtypeStruct((CHANNELS // UNROLL, 2 * UNROLL * KEPT, 256), jnp.bfloat16),
        ),
        scratch_shapes=[
            pltpu.VMEM((BLOCKS * SENT, ROWS), jnp.float32),
            pltpu.VMEM((BLOCKS * CHANNELS, ROWS), jnp.float32),
            pltpu.VMEM((BLOCKS * CHANNELS, ROWS), jnp.float32),
        ],
        name="convolve",
        compiler_params=pltpu.CompilerParams(vmem_limit_bytes=VMEM_GRANT),
    )(signals, *tables)


def complete_body(back_grad_ref, rest_ref, cos_ref, sin_ref, back_ref, last_ref, out_ref, wide_out):
    def step(index, carry):
        cosine = cos_ref[...]
        sine = sin_ref[...]
        total = invert(rest_ref[index], 2 * UNROLL, cosine, sine, back_ref, last_ref)
        for n in range(2 * UNROLL):
            place = index * UNROLL + n // 2
            factor = LAST_SCALE * (ROOT_SCALE if n % 2 else 1.0)
            wide_out[pl.ds(place + CHANNELS * (n % 2), BLOCKS, stride=2 * CHANNELS), :] = (
                total[:, n * 128 : n * 128 + 128] * factor
            )
        return carry

    lax.fori_loop(0, CHANNELS // UNROLL, step, 0)
    wide = wide_out[...].reshape(BLOCKS, 2 * CHANNELS, ROWS).astype(jnp.bfloat16)
    out_ref[:, : 2 * CHANNELS, :] = wide
    out_ref[:, 2 * CHANNELS :, :] = back_grad_ref[...]


def complete(back_grad, rest, tables):
    _, cosine, sine, _, back, last = tables
    return pl.pallas_call(
        complete_body,
        out_shape=jax.ShapeDtypeStruct((BLOCKS, LANES, ROWS), jnp.bfloat16),
        scratch_shapes=[pltpu.VMEM((BLOCKS * 2 * CHANNELS, ROWS), jnp.float32)],
        name="complete",
        compiler_params=pltpu.CompilerParams(vmem_limit_bytes=VMEM_GRANT),
    )(back_grad, rest, cosine, sine, back, last)


def finish_body(back_ref, grad_ref, value_ref, key_ref, query_out, key_out, value_out, filter_out):
    for part in range(8):
        cols = pl.ds(part * 128, 128)

        def turned(place):
            block = back_ref[pl.ds(part * 8, 8), pl.ds(place * 16, 16), :]
            return block.reshape(128, 128).astype(jnp.float32).T

        back = turned(2)
        query_out[:, cols] = (grad_ref[:, cols].astype(jnp.float32) * turned(0)).astype(jnp.bfloat16)
        key_out[:, cols] = (back * value_ref[:, cols].astype(jnp.float32)).astype(jnp.bfloat16)
        value_out[:, cols] = (back * key_ref[:, cols].astype(jnp.float32)).astype(jnp.bfloat16)
        filter_out[:, cols] = turned(1).astype(jnp.bfloat16)


def finish(returned, grad_out, value_proj, gate_key):
    shape = jax.ShapeDtypeStruct(grad_out.shape, jnp.bfloat16)
    return pl.pallas_call(finish_body, out_shape=(shape,) * 4, name="finish", compiler_params=pltpu.CompilerParams(vmem_limit_bytes=VMEM_GRANT))(
        returned, grad_out, value_proj, gate_key
    )


def weight_body(where_ref, value_ref, *refs):
    features, (kept_ref, sent_ref, aligned, pieces) = refs[:8], refs[8:]
    x, ring, place = where_ref[0], where_ref[1], where_ref[2]
    for z in range(2):
        for back in range(4):
            block = value_ref[:, z * 4 + (x - back + 4) % 4]
            aligned[z, :, back * 128 : back * 128 + 128] = block.reshape(512, ROWS)
    for apart in range(4):
        total = None
        for half in range(2):
            source = (ring - apart - 4 * half + 8) % 8
            rows = features[apart + 4 * half]
            rows = jnp.concatenate([rows[back] for back in range(4)], axis=1)
            term = lax.dot_general(
                rows, aligned[source // 4], (((1,), (1,)), ((), ())), preferred_element_type=jnp.float32
            )
            total = term if total is None else total + term
        group = (ring - apart + 8) % 4
        for side in range(2):
            for core in range(2):
                target = ((group % 2) * 2 + side) * 2 + core
                start = side * 128 + core * 64
                pieces[target * 2 + group // 2] = total[start : start + 64].astype(jnp.bfloat16)
    side, core = place // 2, place % 2
    for flip in range(4):
        target = (side ^ flip) * 2
        kept_ref[flip] = pieces[pl.ds((target + core) * 2, 2)]
        sent_ref[flip] = pieces[pl.ds((target + 1 - core) * 2, 2)]


def weight_parts(where, value, features):
    return pl.pallas_call(
        weight_body,
        out_shape=(jax.ShapeDtypeStruct((4, 2, 64, 512), jnp.bfloat16),) * 2,
        in_specs=[pl.BlockSpec(memory_space=pltpu.SMEM)] + [pl.BlockSpec(memory_space=pltpu.VMEM)] * 9,
        scratch_shapes=[
            pltpu.VMEM((2, 512, 512), jnp.bfloat16),
            pltpu.VMEM((16, 64, 512), jnp.bfloat16),
        ],
        name="weight_parts",
        compiler_params=pltpu.CompilerParams(vmem_limit_bytes=VMEM_GRANT),
    )(where, value, *features)


def join_body(kept_ref, received_ref, *outs):
    for flip, out_ref in enumerate(outs):
        total = kept_ref[flip].astype(jnp.float32) + received_ref[flip].astype(jnp.float32)
        out_ref[...] = total.astype(jnp.bfloat16)


def join_cores(kept, received):
    return pl.pallas_call(
        join_body,
        out_shape=(jax.ShapeDtypeStruct((2, 64, 512), jnp.bfloat16),) * 4,
        name="join_cores",
        compiler_params=pltpu.CompilerParams(vmem_limit_bytes=VMEM_GRANT),
    )(kept, received)


def total_body(where_ref, *refs):
    parts, (kept_ref, sent_ref) = refs[:4], refs[4:]
    z = where_ref[3]
    for out_ref, place in ((kept_ref, z), (sent_ref, 1 - z)):
        total = parts[0][place].astype(jnp.float32)
        for part in parts[1:]:
            total = total + part[place].astype(jnp.float32)
        out_ref[...] = total * ROOT_SCALE


def weight_total(where, parts):
    return pl.pallas_call(
        total_body,
        out_shape=(jax.ShapeDtypeStruct((64, 512), jnp.float32),) * 2,
        in_specs=[pl.BlockSpec(memory_space=pltpu.SMEM)] + [pl.BlockSpec(memory_space=pltpu.VMEM)] * 4,
        name="weight_total",
        compiler_params=pltpu.CompilerParams(vmem_limit_bytes=VMEM_GRANT),
    )(where, *parts)


def exchange(array, groups=None):
    return lax.all_to_all(
        array, "seq", split_axis=0, concat_axis=0, tiled=True, axis_index_groups=groups
    )


def ring_step(array, shift):
    return lax.ppermute(array, ("seq", "chan"), along_z(shift))


def shards(layer_input, gate_query, gate_key, value_proj, grad_out, filter_taps):
    tables = [jnp.asarray(table) for table in make_tables()]
    index = lax.axis_index("seq")
    z, y, x, core = index // 32, index // 8 % 4, index // 2 % 4, index % 2
    where = jnp.stack([x, z * 4 + lax.axis_index("chan"), y * 2 + core, z]).astype(jnp.int32)
    pieces = split_features(where, layer_input)
    own = [lax.ppermute(pieces[n], "seq", along_x(n)) for n in range(1, 4)]
    own = jnp.stack([pieces[0]] + own)
    sent = gather_signals(gate_key, value_proj, grad_out, gate_query, filter_taps)
    up, down = ring_step(own, 1), ring_step(own, -1)
    signals = exchange(sent)
    up2, down2 = ring_step(up, 1), ring_step(down, -1)
    back_grad, value, rest = convolve(signals, tables)
    up3, down3, far = ring_step(up2, 1), ring_step(down2, -1), ring_step(up2, 2)
    value = exchange(value, PLANES)
    results = complete(back_grad, rest, tables)
    kept, sent = weight_parts(where, value, (own, up, up2, up3, far, down3, down2, down))
    received = lax.ppermute(sent, "seq", across(1))
    results = exchange(results)
    parts = join_cores(kept, received)
    parts = [parts[0]] + [lax.ppermute(parts[n], "seq", across(2 * n)) for n in range(1, 4)]
    kept, sent = weight_total(where, parts)
    received = lax.ppermute(sent, "seq", opposite())
    grad_query, grad_key, grad_value, grad_filter = finish(results, grad_out, value_proj, gate_key)
    grad_weight = jnp.where(
        z == 0,
        jnp.concatenate([kept, received], axis=1),
        jnp.concatenate([received, kept], axis=1),
    )
    return (grad_query, grad_key, grad_value, grad_filter, grad_weight)


def solution(mesh):
    placed = P("seq", "chan")
    return jax.shard_map(
        shards,
        mesh=mesh,
        in_specs=(placed,) * 6,
        out_specs=(placed,) * 5,
        check_vma=False,
    )
```

```python
import math

import numpy as np

import jax
import jax.numpy as jnp
from jax import lax
from jax.experimental import pallas as pl
from jax.experimental.pallas import tpu as pltpu
from jax.sharding import PartitionSpec as P


BLOCKS = 64
ROWS = 128
CHANNELS = 16
LANES = 3 * CHANNELS
PERIOD = 2 * BLOCKS * ROWS
LAST_SCALE = 1.0 / PERIOD
KEPT = 72
VMEM_GRANT = 12 << 20
ROOT_SCALE = 1.0 / math.sqrt(BLOCKS * ROWS)
SENT = 4 * CHANNELS


def along_x(shift):
    return [(s, s // 8 * 8 + (s // 2 + shift) % 4 * 2 + s % 2) for s in range(64)]


def across(flip):
    pairs = []
    for s in range(64):
        place = (s // 8 % 4 * 2 + s % 2) ^ flip
        pairs.append((s, s // 32 * 32 + place // 2 * 8 + s // 2 % 4 * 2 + place % 2))
    return pairs


def along_z(shift):
    pairs = []
    for flat in range(256):
        s, c = divmod(flat, 4)
        place = (s // 32 * 4 + c + shift) % 8
        pairs.append((flat, (place // 4 * 32 + s % 32) * 4 + place % 4))
    return pairs


def opposite():
    return [(s, (s + 32) % 64) for s in range(64)]


def split_table(table):
    high = table.astype(jnp.bfloat16)
    low = (table - high.astype(np.float64)).astype(jnp.bfloat16)
    return high, low


def make_tables():
    freq = np.arange(KEPT)
    block = np.arange(BLOCKS)
    row = np.arange(ROWS)
    outer = 2.0 * math.pi * (freq[:, None] * block[None, :] % (2 * BLOCKS)) / (2 * BLOCKS)
    first = np.concatenate([np.cos(outer), -np.sin(outer)], axis=0)
    first = np.concatenate(split_table(first), axis=1)
    weight = np.where((freq == 0) | (freq == BLOCKS), 1.0, np.where(freq < BLOCKS, 2.0, 0.0))
    last = np.concatenate([np.cos(outer).T * weight, -np.sin(outer).T * weight], axis=1)
    last = np.concatenate(split_table(last), axis=0)
    twist = 2.0 * math.pi * (freq[:, None] * row[None, :] % PERIOD) / PERIOD
    inner = 2.0 * math.pi * (row[:, None] * row[None, :] % ROWS) / ROWS
    cosine, sine = np.cos(inner), np.sin(inner)
    ahead = np.block([[cosine, -sine], [sine, cosine]])
    return (
        first,
        np.cos(twist).astype(np.float32),
        np.sin(twist).astype(np.float32),
        np.concatenate(split_table(ahead), axis=0),
        np.concatenate(split_table(ahead.T), axis=0),
        last,
    )


def product(left, right):
    return lax.dot_general(left, right, (((1,), (0,)), ((), ())), preferred_element_type=jnp.float32)


WHOLE_GRANT = 60 << 20
STEPS = 4


def gather_body(key_ref, value_ref, grad_ref, query_ref, taps_ref, sent_ref):
    for part in range(8 // STEPS):
        cols = pl.ds(part * 128, 128)
        key = key_ref[:, cols].astype(jnp.float32)
        mixed = key * value_ref[:, cols].astype(jnp.float32)
        gated = grad_ref[:, cols].astype(jnp.float32) * query_ref[:, cols].astype(jnp.float32)
        for place, signal in enumerate((mixed, taps_ref[:, cols].astype(jnp.float32), gated, key)):
            turned = signal.T.astype(jnp.bfloat16)
            sent_ref[pl.ds(part * 8, 8), pl.ds(place * 16, 16), :] = turned.reshape(8, 16, 128)


def gather_signals(gate_key, value_proj, grad_out, gate_query, filter_taps):
    return pl.pallas_call(
        gather_body,
        grid=(STEPS,),
        out_shape=jax.ShapeDtypeStruct((BLOCKS, SENT, ROWS), jnp.bfloat16),
        in_specs=[pl.BlockSpec((ROWS, 1024 // STEPS), lambda i: (0, i))] * 5,
        out_specs=pl.BlockSpec((BLOCKS // STEPS, SENT, ROWS), lambda i: (i, 0, 0)),
        name="gather_signals",
        compiler_params=pltpu.CompilerParams(vmem_limit_bytes=WHOLE_GRANT),
    )(gate_key, value_proj, grad_out, gate_query, filter_taps)


def stage_body(*refs):
    half = len(refs) // 2
    for source, target in zip(refs[:half], refs[half:]):
        target[...] = source[...]


def stage(arrays):
    return pl.pallas_call(
        stage_body,
        out_shape=tuple(jax.ShapeDtypeStruct(array.shape, array.dtype) for array in arrays),
        name="stage",
        compiler_params=pltpu.CompilerParams(vmem_limit_bytes=VMEM_GRANT),
    )(*arrays)


def features_body(where_ref, input_ref, *outs):
    for shift, out_ref in enumerate(outs):
        start = (where_ref[0] + shift) % 4 * 128
        for side in range(2):
            block = input_ref[:, pl.ds(pl.multiple_of(side * 512 + start, 128), 128)]
            out_ref[side * 128 : side * 128 + 128, :] = block.astype(jnp.float32).T.astype(jnp.bfloat16)


def split_features(where, layer_input):
    return pl.pallas_call(
        features_body,
        out_shape=(jax.ShapeDtypeStruct((256, ROWS), jnp.bfloat16),) * 4,
        in_specs=[
            pl.BlockSpec(memory_space=pltpu.SMEM),
            pl.BlockSpec(memory_space=pltpu.VMEM),
        ],
        name="split_features",
        compiler_params=pltpu.CompilerParams(vmem_limit_bytes=VMEM_GRANT),
    )(where, layer_input)


UNROLL = 4


def invert(pairs, number, cosine, sine, back_ref, last_ref):
    rowed = product(jnp.concatenate([pairs, pairs], axis=1), back_ref[...])
    bent = []
    for n in range(number):
        real_part = rowed[n * KEPT : n * KEPT + KEPT, :128]
        other_part = rowed[n * KEPT : n * KEPT + KEPT, 128:]
        bent.append(
            jnp.concatenate(
                [
                    real_part * cosine - other_part * sine,
                    real_part * sine + other_part * cosine,
                ],
                axis=0,
            )
        )
    total = product(last_ref[...], jnp.concatenate(bent, axis=1).astype(jnp.bfloat16))
    return total[:BLOCKS] + total[BLOCKS:]


def convolve_body(
    where_ref, signals_ref, first_ref, cos_ref, sin_ref, ahead_ref, back_ref, last_ref,
    out_ref, rest_ref, *refs,
):
    pieces, (wide_in, wide_out, wide_value, sorted_value) = refs[:8], refs[8:]
    wide_in[...] = signals_ref[...].astype(jnp.float32).reshape(BLOCKS * SENT, ROWS)

    def step(index, carry):
        cosine = cos_ref[...]
        sine = sin_ref[...]
        places = [index * UNROLL + inside for inside in range(UNROLL)]
        rows = jnp.concatenate(
            [
                wide_in[pl.ds(place + CHANNELS * s, BLOCKS, stride=SENT), :]
                for place in places
                for s in range(3)
            ],
            axis=1,
        ).astype(jnp.bfloat16)
        outer = product(first_ref[...], jnp.concatenate([rows, rows], axis=0))
        turned = []
        for n in range(3 * UNROLL):
            real_part = outer[:KEPT, n * 128 : n * 128 + 128]
            other_part = outer[KEPT:, n * 128 : n * 128 + 128]
            turned.append(
                jnp.concatenate(
                    [
                        real_part * cosine + other_part * sine,
                        other_part * cosine - real_part * sine,
                    ],
                    axis=1,
                )
            )
        turned = jnp.concatenate(turned, axis=0).astype(jnp.bfloat16)
        spectra = product(jnp.concatenate([turned, turned], axis=1), ahead_ref[...])
        firsts, rest = [], []
        for n in range(UNROLL):
            parts = [
                (spectra[start : start + KEPT, :128], spectra[start : start + KEPT, 128:])
                for start in range(3 * n * KEPT, (3 * n + 3) * KEPT, KEPT)
            ]
            (mixed_real, mixed_other), (taps_real, taps_other), (gated_real, gated_other) = parts
            firsts.append(
                jnp.concatenate(
                    [
                        gated_real * taps_real + gated_other * taps_other,
                        gated_other * taps_real - gated_real * taps_other,
                    ],
                    axis=1,
                )
            )
            rest.append(
                jnp.concatenate(
                    [
                        mixed_real * taps_real - mixed_other * taps_other,
                        mixed_real * taps_other + mixed_other * taps_real,
                    ],
                    axis=1,
                )
            )
            rest.append(
                jnp.concatenate(
                    [
                        gated_real * mixed_real + gated_other * mixed_other,
                        gated_other * mixed_real - gated_real * mixed_other,
                    ],
                    axis=1,
                )
            )
        rest_ref[index] = jnp.concatenate(rest, axis=0).astype(jnp.bfloat16)
        firsts = jnp.concatenate(firsts, axis=0).astype(jnp.bfloat16)
        total = invert(firsts, UNROLL, cosine, sine, back_ref, last_ref)
        for n, place in enumerate(places):
            result = total[:, n * 128 : n * 128 + 128] * LAST_SCALE
            wide_out[pl.ds(place, BLOCKS, stride=CHANNELS), :] = result
            key = wide_in[pl.ds(place + CHANNELS * 3, BLOCKS, stride=SENT), :]
            wide_value[pl.ds(place, BLOCKS, stride=CHANNELS), :] = (
                result.astype(jnp.bfloat16).astype(jnp.float32) * key
            )
        return carry

    lax.fori_loop(0, CHANNELS // UNROLL, step, 0)
    out_ref[...] = wide_out[...].reshape(BLOCKS, CHANNELS, ROWS).astype(jnp.bfloat16)
    for block in range(BLOCKS):
        tile = wide_value[block * CHANNELS : block * CHANNELS + CHANNELS, :].astype(jnp.bfloat16)
        z, y, x, core = block // 32, block // 8 % 4, block // 2 % 4, block % 2
        sorted_value[y * 2 + core, z * 4 + x] = tile
    for flip, piece in enumerate(pieces):
        piece[...] = sorted_value[where_ref[2] ^ flip]


def convolve(where, signals, tables):
    return pl.pallas_call(
        convolve_body,
        out_shape=(
            jax.ShapeDtypeStruct((BLOCKS, CHANNELS, ROWS), jnp.bfloat16),
            jax.ShapeDtypeStruct((CHANNELS // UNROLL, 2 * UNROLL * KEPT, 256), jnp.bfloat16),
        )
        + (jax.ShapeDtypeStruct((8, CHANNELS, ROWS), jnp.bfloat16),) * 8,
        in_specs=[pl.BlockSpec(memory_space=pltpu.SMEM)] + [pl.BlockSpec(memory_space=pltpu.VMEM)] * 7,
        scratch_shapes=[
            pltpu.VMEM((BLOCKS * SENT, ROWS), jnp.float32),
            pltpu.VMEM((BLOCKS * CHANNELS, ROWS), jnp.float32),
            pltpu.VMEM((BLOCKS * CHANNELS, ROWS), jnp.float32),
            pltpu.VMEM((8, 8, CHANNELS, ROWS), jnp.bfloat16),
        ],
        name="convolve",
        compiler_params=pltpu.CompilerParams(vmem_limit_bytes=VMEM_GRANT),
    )(where, signals, *tables)


def complete_body(back_grad_ref, rest_ref, cos_ref, sin_ref, back_ref, last_ref, out_ref, wide_out):
    def step(index, carry):
        cosine = cos_ref[...]
        sine = sin_ref[...]
        total = invert(rest_ref[index], 2 * UNROLL, cosine, sine, back_ref, last_ref)
        for n in range(2 * UNROLL):
            place = index * UNROLL + n // 2
            factor = LAST_SCALE * (ROOT_SCALE if n % 2 else 1.0)
            wide_out[pl.ds(place + CHANNELS * (n % 2), BLOCKS, stride=2 * CHANNELS), :] = (
                total[:, n * 128 : n * 128 + 128] * factor
            )
        return carry

    lax.fori_loop(0, CHANNELS // UNROLL, step, 0)
    wide = wide_out[...].reshape(BLOCKS, 2 * CHANNELS, ROWS).astype(jnp.bfloat16)
    out_ref[:, : 2 * CHANNELS, :] = wide
    out_ref[:, 2 * CHANNELS :, :] = back_grad_ref[...]


def complete(back_grad, rest, tables):
    _, cosine, sine, _, back, last = tables
    return pl.pallas_call(
        complete_body,
        out_shape=jax.ShapeDtypeStruct((BLOCKS, LANES, ROWS), jnp.bfloat16),
        scratch_shapes=[pltpu.VMEM((BLOCKS * 2 * CHANNELS, ROWS), jnp.float32)],
        name="complete",
        compiler_params=pltpu.CompilerParams(vmem_limit_bytes=VMEM_GRANT),
    )(back_grad, rest, cosine, sine, back, last)


def finish_body(back_ref, grad_ref, value_ref, key_ref, query_out, key_out, value_out, filter_out):
    for part in range(8):
        cols = pl.ds(part * 128, 128)

        def turned(place):
            block = back_ref[pl.ds(part * 8, 8), pl.ds(place * 16, 16), :]
            return block.reshape(128, 128).astype(jnp.float32).T

        back = turned(2)
        query_out[:, cols] = (grad_ref[:, cols].astype(jnp.float32) * turned(0)).astype(jnp.bfloat16)
        key_out[:, cols] = (back * value_ref[:, cols].astype(jnp.float32)).astype(jnp.bfloat16)
        value_out[:, cols] = (back * key_ref[:, cols].astype(jnp.float32)).astype(jnp.bfloat16)
        filter_out[:, cols] = turned(1).astype(jnp.bfloat16)


def finish(returned, grad_out, value_proj, gate_key):
    shape = jax.ShapeDtypeStruct(grad_out.shape, jnp.bfloat16)
    return pl.pallas_call(finish_body, out_shape=(shape,) * 4, name="finish", compiler_params=pltpu.CompilerParams(vmem_limit_bytes=VMEM_GRANT))(
        returned, grad_out, value_proj, gate_key
    )


def bundle_body(*refs):
    for n, piece in enumerate(refs[:8]):
        refs[8][n] = piece[...]


def bundle(pieces):
    return pl.pallas_call(
        bundle_body,
        out_shape=jax.ShapeDtypeStruct((8, 8, CHANNELS, ROWS), jnp.bfloat16),
        name="bundle",
        compiler_params=pltpu.CompilerParams(vmem_limit_bytes=VMEM_GRANT),
    )(*pieces)


def weight_body(where_ref, *refs):
    values, features = refs[:4], refs[4:12]
    kept_ref, sent_ref, aligned, pieces = refs[12:]
    x, ring, place = where_ref[0], where_ref[1], where_ref[2]
    for apart, value_ref in enumerate(values):
        column = (x - apart + 4) % 4
        for flip in range(8):
            origin = place ^ flip
            origin = origin // 2 * 8 + column * 2 + origin % 2
            for z in range(2):
                for back in range(4):
                    aligned[z, origin, :, back * 128 : back * 128 + 128] = value_ref[
                        flip, z * 4 + (x - back + 4) % 4
                    ]
    for apart in range(4):
        total = None
        for half in range(2):
            source = (ring - apart - 4 * half + 8) % 8
            rows = features[apart + 4 * half]
            rows = jnp.concatenate([rows[back] for back in range(4)], axis=1)
            term = lax.dot_general(
                rows,
                aligned[source // 4].reshape(512, 512),
                (((1,), (1,)), ((), ())),
                preferred_element_type=jnp.float32,
            )
            total = term if total is None else total + term
        group = (ring - apart + 8) % 4
        for side in range(2):
            for core in range(2):
                target = ((group % 2) * 2 + side) * 2 + core
                start = side * 128 + core * 64
                pieces[target * 2 + group // 2] = total[start : start + 64].astype(jnp.bfloat16)
    side, core = place // 2, place % 2
    for flip in range(4):
        target = (side ^ flip) * 2
        kept_ref[flip] = pieces[pl.ds((target + core) * 2, 2)]
        sent_ref[flip] = pieces[pl.ds((target + 1 - core) * 2, 2)]


def weight_parts(where, values, features):
    return pl.pallas_call(
        weight_body,
        out_shape=(jax.ShapeDtypeStruct((4, 2, 64, 512), jnp.bfloat16),) * 2,
        in_specs=[pl.BlockSpec(memory_space=pltpu.SMEM)]
        + [pl.BlockSpec(memory_space=pltpu.VMEM)] * 12,
        scratch_shapes=[
            pltpu.VMEM((2, 32, CHANNELS, 512), jnp.bfloat16),
            pltpu.VMEM((16, 64, 512), jnp.bfloat16),
        ],
        name="weight_parts",
        compiler_params=pltpu.CompilerParams(vmem_limit_bytes=VMEM_GRANT),
    )(where, *values, *features)


def join_body(kept_ref, received_ref, *outs):
    for flip, out_ref in enumerate(outs):
        total = kept_ref[flip].astype(jnp.float32) + received_ref[flip].astype(jnp.float32)
        out_ref[...] = total.astype(jnp.bfloat16)


def join_cores(kept, received):
    return pl.pallas_call(
        join_body,
        out_shape=(jax.ShapeDtypeStruct((2, 64, 512), jnp.bfloat16),) * 4,
        name="join_cores",
        compiler_params=pltpu.CompilerParams(vmem_limit_bytes=VMEM_GRANT),
    )(kept, received)


def total_body(where_ref, *refs):
    parts, (kept_ref, sent_ref) = refs[:4], refs[4:]
    z = where_ref[3]
    for out_ref, place in ((kept_ref, z), (sent_ref, 1 - z)):
        total = parts[0][place].astype(jnp.float32)
        for part in parts[1:]:
            total = total + part[place].astype(jnp.float32)
        out_ref[...] = (total * ROOT_SCALE).astype(out_ref.dtype)


def weight_total(where, parts):
    return pl.pallas_call(
        total_body,
        out_shape=(
            jax.ShapeDtypeStruct((64, 512), jnp.float32),
            jax.ShapeDtypeStruct((64, 512), jnp.bfloat16),
        ),
        in_specs=[pl.BlockSpec(memory_space=pltpu.SMEM)] + [pl.BlockSpec(memory_space=pltpu.VMEM)] * 4,
        name="weight_total",
        compiler_params=pltpu.CompilerParams(vmem_limit_bytes=VMEM_GRANT),
    )(where, *parts)


def exchange(array):
    return lax.all_to_all(array, "seq", split_axis=0, concat_axis=0, tiled=True)


def ring_step(array, shift):
    return lax.ppermute(array, ("seq", "chan"), along_z(shift))


def shards(layer_input, gate_query, gate_key, value_proj, grad_out, filter_taps):
    tables = [jnp.asarray(table) for table in make_tables()]
    index = lax.axis_index("seq")
    z, y, x, core = index // 32, index // 8 % 4, index // 2 % 4, index % 2
    where = jnp.stack([x, z * 4 + lax.axis_index("chan"), y * 2 + core, z]).astype(jnp.int32)
    pieces = split_features(where, layer_input)
    own = [lax.ppermute(pieces[n], "seq", along_x(n)) for n in range(1, 4)]
    own = jnp.stack([pieces[0]] + own)
    sent = gather_signals(gate_key, value_proj, grad_out, gate_query, filter_taps)
    up, down = ring_step(own, 1), ring_step(own, -1)
    tables = stage(tables)
    signals = exchange(sent)
    up2, down2 = ring_step(up, 1), ring_step(down, -1)
    back_grad, rest, *pieces = convolve(where, signals, tables)
    pieces = pieces[:1] + [lax.ppermute(pieces[n], "seq", across(n)) for n in range(1, 8)]
    up3, down3, far = ring_step(up2, 1), ring_step(down2, -1), ring_step(up2, 2)
    results = complete(back_grad, rest, tables)
    value = bundle(pieces)
    values = [value] + [lax.ppermute(value, "seq", along_x(n)) for n in range(1, 4)]
    results = exchange(results)
    kept, sent = weight_parts(where, values, (own, up, up2, up3, far, down3, down2, down))
    received = lax.ppermute(sent, "seq", across(1))
    parts = join_cores(kept, received)
    parts = [parts[0]] + [lax.ppermute(parts[n], "seq", across(2 * n)) for n in range(1, 4)]
    kept, sent = weight_total(where, parts)
    received = lax.ppermute(sent, "seq", opposite()).astype(jnp.float32)
    grad_query, grad_key, grad_value, grad_filter = finish(results, grad_out, value_proj, gate_key)
    grad_weight = jnp.where(
        z == 0,
        jnp.concatenate([kept, received], axis=1),
        jnp.concatenate([received, kept], axis=1),
    )
    return (grad_query, grad_key, grad_value, grad_filter, grad_weight)


def solution(mesh):
    placed = P("seq", "chan")
    return jax.shard_map(
        shards,
        mesh=mesh,
        in_specs=(placed,) * 6,
        out_specs=(placed,) * 5,
        check_vma=False,
    )
```

```python
import math

import numpy as np

import jax
import jax.numpy as jnp
from jax import lax
from jax.experimental import pallas as pl
from jax.experimental.pallas import tpu as pltpu
from jax.sharding import PartitionSpec as P


BLOCKS = 64
ROWS = 128
CHANNELS = 16
LANES = 3 * CHANNELS
PERIOD = 2 * BLOCKS * ROWS
LAST_SCALE = 1.0 / PERIOD
KEPT = 72
VMEM_GRANT = 12 << 20
ROOT_SCALE = 1.0 / math.sqrt(BLOCKS * ROWS)
SENT = 4 * CHANNELS


def along_x(shift):
    return [(s, s // 8 * 8 + (s // 2 + shift) % 4 * 2 + s % 2) for s in range(64)]


def across(flip):
    pairs = []
    for s in range(64):
        place = (s // 8 % 4 * 2 + s % 2) ^ flip
        pairs.append((s, s // 32 * 32 + place // 2 * 8 + s // 2 % 4 * 2 + place % 2))
    return pairs


def along_z(shift):
    pairs = []
    for flat in range(256):
        s, c = divmod(flat, 4)
        place = (s // 32 * 4 + c + shift) % 8
        pairs.append((flat, (place // 4 * 32 + s % 32) * 4 + place % 4))
    return pairs


def opposite():
    return [(s, (s + 32) % 64) for s in range(64)]


def split_table(table):
    high = table.astype(jnp.bfloat16)
    low = (table - high.astype(np.float64)).astype(jnp.bfloat16)
    return high, low


def make_tables():
    freq = np.arange(KEPT)
    block = np.arange(BLOCKS)
    row = np.arange(ROWS)
    outer = 2.0 * math.pi * (freq[:, None] * block[None, :] % (2 * BLOCKS)) / (2 * BLOCKS)
    first = np.concatenate([np.cos(outer), -np.sin(outer)], axis=0)
    first = np.concatenate(split_table(first), axis=1)
    weight = np.where((freq == 0) | (freq == BLOCKS), 1.0, np.where(freq < BLOCKS, 2.0, 0.0))
    last = np.concatenate([np.cos(outer).T * weight, -np.sin(outer).T * weight], axis=1)
    last = np.concatenate(split_table(last), axis=0)
    twist = 2.0 * math.pi * (freq[:, None] * row[None, :] % PERIOD) / PERIOD
    inner = 2.0 * math.pi * (row[:, None] * row[None, :] % ROWS) / ROWS
    cosine, sine = np.cos(inner), np.sin(inner)
    ahead = np.block([[cosine, -sine], [sine, cosine]])
    return (
        first,
        np.cos(twist).astype(np.float32),
        np.sin(twist).astype(np.float32),
        np.concatenate(split_table(ahead), axis=0),
        np.concatenate(split_table(ahead.T), axis=0),
        last,
    )


def product(left, right):
    return lax.dot_general(left, right, (((1,), (0,)), ((), ())), preferred_element_type=jnp.float32)


WHOLE_GRANT = 60 << 20
STEPS = 4


def gather_body(key_ref, value_ref, grad_ref, query_ref, taps_ref, sent_ref):
    for part in range(8 // STEPS):
        cols = pl.ds(part * 128, 128)
        key = key_ref[:, cols].astype(jnp.float32)
        mixed = key * value_ref[:, cols].astype(jnp.float32)
        gated = grad_ref[:, cols].astype(jnp.float32) * query_ref[:, cols].astype(jnp.float32)
        for place, signal in enumerate((mixed, taps_ref[:, cols].astype(jnp.float32), gated, key)):
            turned = signal.T.astype(jnp.bfloat16)
            sent_ref[pl.ds(part * 8, 8), pl.ds(place * 16, 16), :] = turned.reshape(8, 16, 128)


def gather_signals(gate_key, value_proj, grad_out, gate_query, filter_taps):
    return pl.pallas_call(
        gather_body,
        grid=(STEPS,),
        out_shape=jax.ShapeDtypeStruct((BLOCKS, SENT, ROWS), jnp.bfloat16),
        in_specs=[pl.BlockSpec((ROWS, 1024 // STEPS), lambda i: (0, i))] * 5,
        out_specs=pl.BlockSpec((BLOCKS // STEPS, SENT, ROWS), lambda i: (i, 0, 0)),
        name="gather_signals",
        compiler_params=pltpu.CompilerParams(vmem_limit_bytes=WHOLE_GRANT),
    )(gate_key, value_proj, grad_out, gate_query, filter_taps)


def stage_body(*refs):
    half = len(refs) // 2
    for source, target in zip(refs[:half], refs[half:]):
        target[...] = source[...]


def stage(arrays):
    return pl.pallas_call(
        stage_body,
        out_shape=tuple(jax.ShapeDtypeStruct(array.shape, array.dtype) for array in arrays),
        name="stage",
        compiler_params=pltpu.CompilerParams(vmem_limit_bytes=VMEM_GRANT),
    )(*arrays)


def features_body(where_ref, input_ref, *outs):
    for shift, out_ref in enumerate(outs):
        start = (where_ref[0] + shift) % 4 * 128
        for side in range(2):
            block = input_ref[:, pl.ds(pl.multiple_of(side * 512 + start, 128), 128)]
            out_ref[side * 128 : side * 128 + 128, :] = block.astype(jnp.float32).T.astype(jnp.bfloat16)


def split_features(where, layer_input):
    return pl.pallas_call(
        features_body,
        out_shape=(jax.ShapeDtypeStruct((256, ROWS), jnp.bfloat16),) * 4,
        in_specs=[
            pl.BlockSpec(memory_space=pltpu.SMEM),
            pl.BlockSpec(memory_space=pltpu.VMEM),
        ],
        name="split_features",
        compiler_params=pltpu.CompilerParams(vmem_limit_bytes=VMEM_GRANT),
    )(where, layer_input)


UNROLL = 4


def invert(pairs, number, cosine, sine, back_ref, last_ref):
    rowed = product(jnp.concatenate([pairs, pairs], axis=1), back_ref[...])
    bent = []
    for n in range(number):
        real_part = rowed[n * KEPT : n * KEPT + KEPT, :128]
        other_part = rowed[n * KEPT : n * KEPT + KEPT, 128:]
        bent.append(
            jnp.concatenate(
                [
                    real_part * cosine - other_part * sine,
                    real_part * sine + other_part * cosine,
                ],
                axis=0,
            )
        )
    total = product(last_ref[...], jnp.concatenate(bent, axis=1).astype(jnp.bfloat16))
    return total[:BLOCKS] + total[BLOCKS:]


def convolve_body(
    where_ref, signals_ref, first_ref, cos_ref, sin_ref, ahead_ref, back_ref, last_ref,
    out_ref, rest_ref, *refs,
):
    pieces, (wide_in, wide_out, wide_value, sorted_value) = refs[:8], refs[8:]
    wide_in[...] = signals_ref[...].astype(jnp.float32).reshape(BLOCKS * SENT, ROWS)

    def step(index, carry):
        cosine = cos_ref[...]
        sine = sin_ref[...]
        places = [index * UNROLL + inside for inside in range(UNROLL)]
        rows = jnp.concatenate(
            [
                wide_in[pl.ds(place + CHANNELS * s, BLOCKS, stride=SENT), :]
                for place in places
                for s in range(3)
            ],
            axis=1,
        ).astype(jnp.bfloat16)
        outer = product(first_ref[...], jnp.concatenate([rows, rows], axis=0))
        turned = []
        for n in range(3 * UNROLL):
            real_part = outer[:KEPT, n * 128 : n * 128 + 128]
            other_part = outer[KEPT:, n * 128 : n * 128 + 128]
            turned.append(
                jnp.concatenate(
                    [
                        real_part * cosine + other_part * sine,
                        other_part * cosine - real_part * sine,
                    ],
                    axis=1,
                )
            )
        turned = jnp.concatenate(turned, axis=0).astype(jnp.bfloat16)
        spectra = product(jnp.concatenate([turned, turned], axis=1), ahead_ref[...])
        firsts, rest = [], []
        for n in range(UNROLL):
            parts = [
                (spectra[start : start + KEPT, :128], spectra[start : start + KEPT, 128:])
                for start in range(3 * n * KEPT, (3 * n + 3) * KEPT, KEPT)
            ]
            (mixed_real, mixed_other), (taps_real, taps_other), (gated_real, gated_other) = parts
            firsts.append(
                jnp.concatenate(
                    [
                        gated_real * taps_real + gated_other * taps_other,
                        gated_other * taps_real - gated_real * taps_other,
                    ],
                    axis=1,
                )
            )
            rest.append(
                jnp.concatenate(
                    [
                        mixed_real * taps_real - mixed_other * taps_other,
                        mixed_real * taps_other + mixed_other * taps_real,
                    ],
                    axis=1,
                )
            )
            rest.append(
                jnp.concatenate(
                    [
                        gated_real * mixed_real + gated_other * mixed_other,
                        gated_other * mixed_real - gated_real * mixed_other,
                    ],
                    axis=1,
                )
            )
        rest_ref[index] = jnp.concatenate(rest, axis=0).astype(jnp.bfloat16)
        firsts = jnp.concatenate(firsts, axis=0).astype(jnp.bfloat16)
        total = invert(firsts, UNROLL, cosine, sine, back_ref, last_ref)
        for n, place in enumerate(places):
            result = total[:, n * 128 : n * 128 + 128] * LAST_SCALE
            wide_out[pl.ds(place, BLOCKS, stride=CHANNELS), :] = result
            key = wide_in[pl.ds(place + CHANNELS * 3, BLOCKS, stride=SENT), :]
            wide_value[pl.ds(place, BLOCKS, stride=CHANNELS), :] = (
                result.astype(jnp.bfloat16).astype(jnp.float32) * key
            )
        return carry

    lax.fori_loop(0, CHANNELS // UNROLL, step, 0)
    out_ref[...] = wide_out[...].reshape(BLOCKS, CHANNELS, ROWS).astype(jnp.bfloat16)
    for block in range(BLOCKS):
        tile = wide_value[block * CHANNELS : block * CHANNELS + CHANNELS, :].astype(jnp.bfloat16)
        z, y, x, core = block // 32, block // 8 % 4, block // 2 % 4, block % 2
        sorted_value[y * 2 + core, z * 4 + x] = tile
    for flip, piece in enumerate(pieces):
        piece[...] = sorted_value[where_ref[2] ^ flip]


def convolve(where, signals, tables):
    return pl.pallas_call(
        convolve_body,
        out_shape=(
            jax.ShapeDtypeStruct((BLOCKS, CHANNELS, ROWS), jnp.bfloat16),
            jax.ShapeDtypeStruct((CHANNELS // UNROLL, 2 * UNROLL * KEPT, 256), jnp.bfloat16),
        )
        + (jax.ShapeDtypeStruct((8, CHANNELS, ROWS), jnp.bfloat16),) * 8,
        in_specs=[pl.BlockSpec(memory_space=pltpu.SMEM)] + [pl.BlockSpec(memory_space=pltpu.VMEM)] * 7,
        scratch_shapes=[
            pltpu.VMEM((BLOCKS * SENT, ROWS), jnp.float32),
            pltpu.VMEM((BLOCKS * CHANNELS, ROWS), jnp.float32),
            pltpu.VMEM((BLOCKS * CHANNELS, ROWS), jnp.float32),
            pltpu.VMEM((8, 8, CHANNELS, ROWS), jnp.bfloat16),
        ],
        name="convolve",
        compiler_params=pltpu.CompilerParams(vmem_limit_bytes=VMEM_GRANT),
    )(where, signals, *tables)


def complete_body(back_grad_ref, rest_ref, cos_ref, sin_ref, back_ref, last_ref, out_ref, wide_out):
    def step(index, carry):
        cosine = cos_ref[...]
        sine = sin_ref[...]
        total = invert(rest_ref[index], 2 * UNROLL, cosine, sine, back_ref, last_ref)
        for n in range(2 * UNROLL):
            place = index * UNROLL + n // 2
            factor = LAST_SCALE * (ROOT_SCALE if n % 2 else 1.0)
            wide_out[pl.ds(place + CHANNELS * (n % 2), BLOCKS, stride=2 * CHANNELS), :] = (
                total[:, n * 128 : n * 128 + 128] * factor
            )
        return carry

    lax.fori_loop(0, CHANNELS // UNROLL, step, 0)
    wide = wide_out[...].reshape(BLOCKS, 2 * CHANNELS, ROWS).astype(jnp.bfloat16)
    out_ref[:, : 2 * CHANNELS, :] = wide
    out_ref[:, 2 * CHANNELS :, :] = back_grad_ref[...]


def complete(back_grad, rest, tables):
    _, cosine, sine, _, back, last = tables
    return pl.pallas_call(
        complete_body,
        out_shape=jax.ShapeDtypeStruct((BLOCKS, LANES, ROWS), jnp.bfloat16),
        scratch_shapes=[pltpu.VMEM((BLOCKS * 2 * CHANNELS, ROWS), jnp.float32)],
        name="complete",
        compiler_params=pltpu.CompilerParams(vmem_limit_bytes=VMEM_GRANT),
    )(back_grad, rest, cosine, sine, back, last)


def finish_body(back_ref, grad_ref, value_ref, key_ref, query_out, key_out, value_out, filter_out):
    for part in range(8):
        cols = pl.ds(part * 128, 128)

        def turned(place):
            block = back_ref[pl.ds(part * 8, 8), pl.ds(place * 16, 16), :]
            return block.reshape(128, 128).astype(jnp.float32).T

        back = turned(2)
        query_out[:, cols] = (grad_ref[:, cols].astype(jnp.float32) * turned(0)).astype(jnp.bfloat16)
        key_out[:, cols] = (back * value_ref[:, cols].astype(jnp.float32)).astype(jnp.bfloat16)
        value_out[:, cols] = (back * key_ref[:, cols].astype(jnp.float32)).astype(jnp.bfloat16)
        filter_out[:, cols] = turned(1).astype(jnp.bfloat16)


def finish(returned, grad_out, value_proj, gate_key):
    shape = jax.ShapeDtypeStruct(grad_out.shape, jnp.bfloat16)
    return pl.pallas_call(finish_body, out_shape=(shape,) * 4, name="finish", compiler_params=pltpu.CompilerParams(vmem_limit_bytes=VMEM_GRANT))(
        returned, grad_out, value_proj, gate_key
    )


def bundle_body(*refs):
    for n, piece in enumerate(refs[:8]):
        refs[8][n] = piece[...]


def bundle(pieces):
    return pl.pallas_call(
        bundle_body,
        out_shape=jax.ShapeDtypeStruct((8, 8, CHANNELS, ROWS), jnp.bfloat16),
        name="bundle",
        compiler_params=pltpu.CompilerParams(vmem_limit_bytes=VMEM_GRANT),
    )(*pieces)


def weight_body(where_ref, *refs):
    values, features, far_rest = refs[:4], refs[4:12], refs[12]
    kept_ref, sent_ref, aligned, pieces = refs[13:]
    x, ring, place = where_ref[0], where_ref[1], where_ref[2]
    for apart, value_ref in enumerate(values):
        column = (x - apart + 4) % 4
        for flip in range(8):
            origin = place ^ flip
            origin = origin // 2 * 8 + column * 2 + origin % 2
            for z in range(2):
                for back in range(4):
                    aligned[z, origin, :, back * 128 : back * 128 + 128] = value_ref[
                        flip, z * 4 + (x - back + 4) % 4
                    ]
    for apart in range(4):
        total = None
        for half in range(2):
            source = (ring - apart - 4 * half + 8) % 8
            rows = features[apart + 4 * half]
            if apart + 4 * half == 4:
                rows = [rows[0], rows[1], far_rest[0], far_rest[1]]
            else:
                rows = [rows[back] for back in range(4)]
            rows = jnp.concatenate(rows, axis=1)
            term = lax.dot_general(
                rows,
                aligned[source // 4].reshape(512, 512),
                (((1,), (1,)), ((), ())),
                preferred_element_type=jnp.float32,
            )
            total = term if total is None else total + term
        group = (ring - apart + 8) % 4
        for side in range(2):
            for core in range(2):
                target = ((group % 2) * 2 + side) * 2 + core
                start = side * 128 + core * 64
                pieces[target * 2 + group // 2] = total[start : start + 64].astype(jnp.bfloat16)
    side, core = place // 2, place % 2
    for flip in range(4):
        target = (side ^ flip) * 2
        kept_ref[flip] = pieces[pl.ds((target + core) * 2, 2)]
        sent_ref[flip] = pieces[pl.ds((target + 1 - core) * 2, 2)]


def weight_parts(where, values, features):
    return pl.pallas_call(
        weight_body,
        out_shape=(jax.ShapeDtypeStruct((4, 2, 64, 512), jnp.bfloat16),) * 2,
        in_specs=[pl.BlockSpec(memory_space=pltpu.SMEM)]
        + [pl.BlockSpec(memory_space=pltpu.VMEM)] * 13,
        scratch_shapes=[
            pltpu.VMEM((2, 32, CHANNELS, 512), jnp.bfloat16),
            pltpu.VMEM((16, 64, 512), jnp.bfloat16),
        ],
        name="weight_parts",
        compiler_params=pltpu.CompilerParams(vmem_limit_bytes=VMEM_GRANT),
    )(where, *values, *features)


def join_body(kept_ref, received_ref, *outs):
    for flip, out_ref in enumerate(outs):
        total = kept_ref[flip].astype(jnp.float32) + received_ref[flip].astype(jnp.float32)
        out_ref[...] = total.astype(jnp.bfloat16)


def join_cores(kept, received):
    return pl.pallas_call(
        join_body,
        out_shape=(jax.ShapeDtypeStruct((2, 64, 512), jnp.bfloat16),) * 4,
        name="join_cores",
        compiler_params=pltpu.CompilerParams(vmem_limit_bytes=VMEM_GRANT),
    )(kept, received)


def total_body(where_ref, *refs):
    parts, (kept_ref, sent_ref) = refs[:4], refs[4:]
    z = where_ref[3]
    for out_ref, place in ((kept_ref, z), (sent_ref, 1 - z)):
        total = parts[0][place].astype(jnp.float32)
        for part in parts[1:]:
            total = total + part[place].astype(jnp.float32)
        out_ref[...] = (total * ROOT_SCALE).astype(out_ref.dtype)


def weight_total(where, parts):
    return pl.pallas_call(
        total_body,
        out_shape=(
            jax.ShapeDtypeStruct((64, 512), jnp.float32),
            jax.ShapeDtypeStruct((64, 512), jnp.bfloat16),
        ),
        in_specs=[pl.BlockSpec(memory_space=pltpu.SMEM)] + [pl.BlockSpec(memory_space=pltpu.VMEM)] * 4,
        name="weight_total",
        compiler_params=pltpu.CompilerParams(vmem_limit_bytes=VMEM_GRANT),
    )(where, *parts)


def exchange(array):
    return lax.all_to_all(array, "seq", split_axis=0, concat_axis=0, tiled=True)


def ring_step(array, shift):
    return lax.ppermute(array, ("seq", "chan"), along_z(shift))


def shards(layer_input, gate_query, gate_key, value_proj, grad_out, filter_taps):
    tables = [jnp.asarray(table) for table in make_tables()]
    index = lax.axis_index("seq")
    z, y, x, core = index // 32, index // 8 % 4, index // 2 % 4, index % 2
    where = jnp.stack([x, z * 4 + lax.axis_index("chan"), y * 2 + core, z]).astype(jnp.int32)
    pieces = split_features(where, layer_input)
    own = [lax.ppermute(pieces[n], "seq", along_x(n)) for n in range(1, 4)]
    own = jnp.stack([pieces[0]] + own)
    sent = gather_signals(gate_key, value_proj, grad_out, gate_query, filter_taps)
    up, down = ring_step(own, 1), ring_step(own, -1)
    tables = stage(tables)
    signals = exchange(sent)
    up2, down2 = ring_step(up, 1), ring_step(down, -1)
    back_grad, rest, *pieces = convolve(where, signals, tables)
    pieces = pieces[:1] + [lax.ppermute(pieces[n], "seq", across(n)) for n in range(1, 8)]
    up3, down3 = ring_step(up2, 1), ring_step(down2, -1)
    far, far_rest = ring_step(up2[:2], 2), ring_step(down2[2:], -2)
    results = complete(back_grad, rest, tables)
    value = bundle(pieces)
    values = [value] + [lax.ppermute(value, "seq", along_x(n)) for n in range(1, 4)]
    results = exchange(results)
    kept, sent = weight_parts(where, values, (own, up, up2, up3, far, down3, down2, down, far_rest))
    received = lax.ppermute(sent, "seq", across(1))
    parts = join_cores(kept, received)
    parts = [parts[0]] + [lax.ppermute(parts[n], "seq", across(2 * n)) for n in range(1, 4)]
    kept, sent = weight_total(where, parts)
    received = lax.ppermute(sent, "seq", opposite()).astype(jnp.float32)
    grad_query, grad_key, grad_value, grad_filter = finish(results, grad_out, value_proj, gate_key)
    grad_weight = jnp.where(
        z == 0,
        jnp.concatenate([kept, received], axis=1),
        jnp.concatenate([received, kept], axis=1),
    )
    return (grad_query, grad_key, grad_value, grad_filter, grad_weight)


def solution(mesh):
    placed = P("seq", "chan")
    return jax.shard_map(
        shards,
        mesh=mesh,
        in_specs=(placed,) * 6,
        out_specs=(placed,) * 5,
        check_vma=False,
    )
```

```python
import math

import numpy as np

import jax
import jax.numpy as jnp
from jax import lax
from jax.experimental import pallas as pl
from jax.experimental.pallas import tpu as pltpu
from jax.sharding import PartitionSpec as P


BLOCKS = 64
ROWS = 128
CHANNELS = 16
LANES = 3 * CHANNELS
PERIOD = 2 * BLOCKS * ROWS
LAST_SCALE = 1.0 / PERIOD
KEPT = 72
VMEM_GRANT = 12 << 20
ROOT_SCALE = 1.0 / math.sqrt(BLOCKS * ROWS)
SENT = 4 * CHANNELS


def along_x(shift):
    return [(s, s // 8 * 8 + (s // 2 + shift) % 4 * 2 + s % 2) for s in range(64)]


def across(flip):
    pairs = []
    for s in range(64):
        place = (s // 8 % 4 * 2 + s % 2) ^ flip
        pairs.append((s, s // 32 * 32 + place // 2 * 8 + s // 2 % 4 * 2 + place % 2))
    return pairs


def along_z(shift):
    pairs = []
    for flat in range(256):
        s, c = divmod(flat, 4)
        place = (s // 32 * 4 + c + shift) % 8
        pairs.append((flat, (place // 4 * 32 + s % 32) * 4 + place % 4))
    return pairs


def opposite():
    return [(s, (s + 32) % 64) for s in range(64)]


def split_table(table):
    high = table.astype(jnp.bfloat16)
    low = (table - high.astype(np.float64)).astype(jnp.bfloat16)
    return high, low


def make_tables():
    freq = np.arange(KEPT)
    block = np.arange(BLOCKS)
    row = np.arange(ROWS)
    outer = 2.0 * math.pi * (freq[:, None] * block[None, :] % (2 * BLOCKS)) / (2 * BLOCKS)
    first = np.concatenate([np.cos(outer), -np.sin(outer)], axis=0)
    first = np.concatenate(split_table(first), axis=1)
    weight = np.where((freq == 0) | (freq == BLOCKS), 1.0, np.where(freq < BLOCKS, 2.0, 0.0))
    last = np.concatenate([np.cos(outer).T * weight, -np.sin(outer).T * weight], axis=1)
    last = np.concatenate(split_table(last), axis=0)
    twist = 2.0 * math.pi * (freq[:, None] * row[None, :] % PERIOD) / PERIOD
    inner = 2.0 * math.pi * (row[:, None] * row[None, :] % ROWS) / ROWS
    cosine, sine = np.cos(inner), np.sin(inner)
    ahead = np.block([[cosine, -sine], [sine, cosine]])
    return (
        first,
        np.cos(twist).astype(np.float32),
        np.sin(twist).astype(np.float32),
        np.concatenate(split_table(ahead), axis=0),
        np.concatenate(split_table(ahead.T), axis=0),
        last,
    )


def product(left, right):
    return lax.dot_general(left, right, (((1,), (0,)), ((), ())), preferred_element_type=jnp.float32)


WHOLE_GRANT = 60 << 20


def gather_body(key_ref, value_ref, grad_ref, query_ref, taps_ref, sent_ref):
    for part in range(8):
        cols = pl.ds(part * 128, 128)
        key = key_ref[:, cols].astype(jnp.float32)
        mixed = key * value_ref[:, cols].astype(jnp.float32)
        gated = grad_ref[:, cols].astype(jnp.float32) * query_ref[:, cols].astype(jnp.float32)
        for place, signal in enumerate((mixed, taps_ref[:, cols].astype(jnp.float32), gated, key)):
            turned = signal.T.astype(jnp.bfloat16)
            sent_ref[pl.ds(part * 8, 8), pl.ds(place * 16, 16), :] = turned.reshape(8, 16, 128)


def gather_signals(gate_key, value_proj, grad_out, gate_query, filter_taps):
    return pl.pallas_call(
        gather_body,
        out_shape=jax.ShapeDtypeStruct((BLOCKS, SENT, ROWS), jnp.bfloat16),
        name="gather_signals",
        compiler_params=pltpu.CompilerParams(vmem_limit_bytes=WHOLE_GRANT),
    )(gate_key, value_proj, grad_out, gate_query, filter_taps)


def stage_body(*refs):
    half = len(refs) // 2
    for source, target in zip(refs[:half], refs[half:]):
        target[...] = source[...]


def stage(arrays):
    return pl.pallas_call(
        stage_body,
        out_shape=tuple(jax.ShapeDtypeStruct(array.shape, array.dtype) for array in arrays),
        name="stage",
        compiler_params=pltpu.CompilerParams(vmem_limit_bytes=VMEM_GRANT),
    )(*arrays)


def features_body(where_ref, input_ref, *outs):
    for shift, out_ref in enumerate(outs):
        start = (where_ref[0] + shift) % 4 * 128
        for side in range(2):
            block = input_ref[:, pl.ds(pl.multiple_of(side * 512 + start, 128), 128)]
            out_ref[side * 128 : side * 128 + 128, :] = block.astype(jnp.float32).T.astype(jnp.bfloat16)


def split_features(where, layer_input):
    return pl.pallas_call(
        features_body,
        out_shape=(jax.ShapeDtypeStruct((256, ROWS), jnp.bfloat16),) * 4,
        in_specs=[
            pl.BlockSpec(memory_space=pltpu.SMEM),
            pl.BlockSpec(memory_space=pltpu.VMEM),
        ],
        name="split_features",
        compiler_params=pltpu.CompilerParams(vmem_limit_bytes=VMEM_GRANT),
    )(where, layer_input)


UNROLL = 4


def invert(pairs, number, cosine, sine, back_ref, last_ref):
    rowed = product(jnp.concatenate([pairs, pairs], axis=1), back_ref[...])
    bent = []
    for n in range(number):
        real_part = rowed[n * KEPT : n * KEPT + KEPT, :128]
        other_part = rowed[n * KEPT : n * KEPT + KEPT, 128:]
        bent.append(
            jnp.concatenate(
                [
                    real_part * cosine - other_part * sine,
                    real_part * sine + other_part * cosine,
                ],
                axis=0,
            )
        )
    total = product(last_ref[...], jnp.concatenate(bent, axis=1).astype(jnp.bfloat16))
    return total[:BLOCKS] + total[BLOCKS:]


def convolve_body(
    where_ref, signals_ref, first_ref, cos_ref, sin_ref, ahead_ref, back_ref, last_ref,
    out_ref, rest_ref, *refs,
):
    pieces, (wide_in, wide_out, wide_value, sorted_value) = refs[:8], refs[8:]
    wide_in[...] = signals_ref[...].astype(jnp.float32).reshape(BLOCKS * SENT, ROWS)

    def step(index, carry):
        cosine = cos_ref[...]
        sine = sin_ref[...]
        places = [index * UNROLL + inside for inside in range(UNROLL)]
        rows = jnp.concatenate(
            [
                wide_in[pl.ds(place + CHANNELS * s, BLOCKS, stride=SENT), :]
                for place in places
                for s in range(3)
            ],
            axis=1,
        ).astype(jnp.bfloat16)
        outer = product(first_ref[...], jnp.concatenate([rows, rows], axis=0))
        turned = []
        for n in range(3 * UNROLL):
            real_part = outer[:KEPT, n * 128 : n * 128 + 128]
            other_part = outer[KEPT:, n * 128 : n * 128 + 128]
            turned.append(
                jnp.concatenate(
                    [
                        real_part * cosine + other_part * sine,
                        other_part * cosine - real_part * sine,
                    ],
                    axis=1,
                )
            )
        turned = jnp.concatenate(turned, axis=0).astype(jnp.bfloat16)
        spectra = product(jnp.concatenate([turned, turned], axis=1), ahead_ref[...])
        firsts, rest = [], []
        for n in range(UNROLL):
            parts = [
                (spectra[start : start + KEPT, :128], spectra[start : start + KEPT, 128:])
                for start in range(3 * n * KEPT, (3 * n + 3) * KEPT, KEPT)
            ]
            (mixed_real, mixed_other), (taps_real, taps_other), (gated_real, gated_other) = parts
            firsts.append(
                jnp.concatenate(
                    [
                        gated_real * taps_real + gated_other * taps_other,
                        gated_other * taps_real - gated_real * taps_other,
                    ],
                    axis=1,
                )
            )
            rest.append(
                jnp.concatenate(
                    [
                        mixed_real * taps_real - mixed_other * taps_other,
                        mixed_real * taps_other + mixed_other * taps_real,
                    ],
                    axis=1,
                )
            )
            rest.append(
                jnp.concatenate(
                    [
                        gated_real * mixed_real + gated_other * mixed_other,
                        gated_other * mixed_real - gated_real * mixed_other,
                    ],
                    axis=1,
                )
            )
        rest_ref[index] = jnp.concatenate(rest, axis=0).astype(jnp.bfloat16)
        firsts = jnp.concatenate(firsts, axis=0).astype(jnp.bfloat16)
        total = invert(firsts, UNROLL, cosine, sine, back_ref, last_ref)
        for n, place in enumerate(places):
            result = total[:, n * 128 : n * 128 + 128] * LAST_SCALE
            wide_out[pl.ds(place, BLOCKS, stride=CHANNELS), :] = result
            key = wide_in[pl.ds(place + CHANNELS * 3, BLOCKS, stride=SENT), :]
            wide_value[pl.ds(place, BLOCKS, stride=CHANNELS), :] = (
                result.astype(jnp.bfloat16).astype(jnp.float32) * key
            )
        return carry

    lax.fori_loop(0, CHANNELS // UNROLL, step, 0)
    out_ref[...] = wide_out[...].reshape(BLOCKS, CHANNELS, ROWS).astype(jnp.bfloat16)
    for block in range(BLOCKS):
        tile = wide_value[block * CHANNELS : block * CHANNELS + CHANNELS, :].astype(jnp.bfloat16)
        z, y, x, core = block // 32, block // 8 % 4, block // 2 % 4, block % 2
        sorted_value[y * 2 + core, z * 4 + x] = tile
    for flip, piece in enumerate(pieces):
        piece[...] = sorted_value[where_ref[2] ^ flip]


def convolve(where, signals, tables):
    return pl.pallas_call(
        convolve_body,
        out_shape=(
            jax.ShapeDtypeStruct((BLOCKS, CHANNELS, ROWS), jnp.bfloat16),
            jax.ShapeDtypeStruct((CHANNELS // UNROLL, 2 * UNROLL * KEPT, 256), jnp.bfloat16),
        )
        + (jax.ShapeDtypeStruct((8, CHANNELS, ROWS), jnp.bfloat16),) * 8,
        in_specs=[pl.BlockSpec(memory_space=pltpu.SMEM)] + [pl.BlockSpec(memory_space=pltpu.VMEM)] * 7,
        scratch_shapes=[
            pltpu.VMEM((BLOCKS * SENT, ROWS), jnp.float32),
            pltpu.VMEM((BLOCKS * CHANNELS, ROWS), jnp.float32),
            pltpu.VMEM((BLOCKS * CHANNELS, ROWS), jnp.float32),
            pltpu.VMEM((8, 8, CHANNELS, ROWS), jnp.bfloat16),
        ],
        name="convolve",
        compiler_params=pltpu.CompilerParams(vmem_limit_bytes=VMEM_GRANT),
    )(where, signals, *tables)


def complete_body(back_grad_ref, rest_ref, cos_ref, sin_ref, back_ref, last_ref, out_ref, wide_out):
    def step(index, carry):
        cosine = cos_ref[...]
        sine = sin_ref[...]
        total = invert(rest_ref[index], 2 * UNROLL, cosine, sine, back_ref, last_ref)
        for n in range(2 * UNROLL):
            place = index * UNROLL + n // 2
            factor = LAST_SCALE * (ROOT_SCALE if n % 2 else 1.0)
            wide_out[pl.ds(place + CHANNELS * (n % 2), BLOCKS, stride=2 * CHANNELS), :] = (
                total[:, n * 128 : n * 128 + 128] * factor
            )
        return carry

    lax.fori_loop(0, CHANNELS // UNROLL, step, 0)
    wide = wide_out[...].reshape(BLOCKS, 2 * CHANNELS, ROWS).astype(jnp.bfloat16)
    out_ref[:, : 2 * CHANNELS, :] = wide
    out_ref[:, 2 * CHANNELS :, :] = back_grad_ref[...]


def complete(back_grad, rest, tables):
    _, cosine, sine, _, back, last = tables
    return pl.pallas_call(
        complete_body,
        out_shape=jax.ShapeDtypeStruct((BLOCKS, LANES, ROWS), jnp.bfloat16),
        scratch_shapes=[pltpu.VMEM((BLOCKS * 2 * CHANNELS, ROWS), jnp.float32)],
        name="complete",
        compiler_params=pltpu.CompilerParams(vmem_limit_bytes=VMEM_GRANT),
    )(back_grad, rest, cosine, sine, back, last)


def finish_body(back_ref, grad_ref, value_ref, key_ref, query_out, key_out, value_out, filter_out):
    for part in range(8):
        cols = pl.ds(part * 128, 128)

        def turned(place):
            block = back_ref[pl.ds(part * 8, 8), pl.ds(place * 16, 16), :]
            return block.reshape(128, 128).astype(jnp.float32).T

        back = turned(2)
        query_out[:, cols] = (grad_ref[:, cols].astype(jnp.float32) * turned(0)).astype(jnp.bfloat16)
        key_out[:, cols] = (back * value_ref[:, cols].astype(jnp.float32)).astype(jnp.bfloat16)
        value_out[:, cols] = (back * key_ref[:, cols].astype(jnp.float32)).astype(jnp.bfloat16)
        filter_out[:, cols] = turned(1).astype(jnp.bfloat16)


def finish(returned, grad_out, value_proj, gate_key):
    shape = jax.ShapeDtypeStruct(grad_out.shape, jnp.bfloat16)
    return pl.pallas_call(finish_body, out_shape=(shape,) * 4, name="finish", compiler_params=pltpu.CompilerParams(vmem_limit_bytes=VMEM_GRANT))(
        returned, grad_out, value_proj, gate_key
    )


def bundle_body(*refs):
    for n, piece in enumerate(refs[:8]):
        refs[8][n] = piece[...]


def bundle(pieces):
    return pl.pallas_call(
        bundle_body,
        out_shape=jax.ShapeDtypeStruct((8, 8, CHANNELS, ROWS), jnp.bfloat16),
        name="bundle",
        compiler_params=pltpu.CompilerParams(vmem_limit_bytes=VMEM_GRANT),
    )(*pieces)


def weight_body(where_ref, *refs):
    values, features, far_rest = refs[:4], refs[4:12], refs[12]
    kept_ref, sent_ref, aligned, pieces = refs[13:]
    x, ring, place = where_ref[0], where_ref[1], where_ref[2]
    for apart, value_ref in enumerate(values):
        column = (x - apart + 4) % 4
        for flip in range(8):
            origin = place ^ flip
            origin = origin // 2 * 8 + column * 2 + origin % 2
            for z in range(2):
                for back in range(4):
                    aligned[z, origin, :, back * 128 : back * 128 + 128] = value_ref[
                        flip, z * 4 + (x - back + 4) % 4
                    ]
    for apart in range(4):
        total = None
        for half in range(2):
            source = (ring - apart - 4 * half + 8) % 8
            rows = features[apart + 4 * half]
            if apart + 4 * half == 4:
                rows = [rows[0], rows[1], far_rest[0], far_rest[1]]
            else:
                rows = [rows[back] for back in range(4)]
            rows = jnp.concatenate(rows, axis=1)
            term = lax.dot_general(
                rows,
                aligned[source // 4].reshape(512, 512),
                (((1,), (1,)), ((), ())),
                preferred_element_type=jnp.float32,
            )
            total = term if total is None else total + term
        group = (ring - apart + 8) % 4
        for side in range(2):
            for core in range(2):
                target = ((group % 2) * 2 + side) * 2 + core
                start = side * 128 + core * 64
                pieces[target * 2 + group // 2] = total[start : start + 64].astype(jnp.bfloat16)
    side, core = place // 2, place % 2
    for flip in range(4):
        target = (side ^ flip) * 2
        kept_ref[flip] = pieces[pl.ds((target + core) * 2, 2)]
        sent_ref[flip] = pieces[pl.ds((target + 1 - core) * 2, 2)]


def weight_parts(where, values, features):
    return pl.pallas_call(
        weight_body,
        out_shape=(jax.ShapeDtypeStruct((4, 2, 64, 512), jnp.bfloat16),) * 2,
        in_specs=[pl.BlockSpec(memory_space=pltpu.SMEM)]
        + [pl.BlockSpec(memory_space=pltpu.VMEM)] * 13,
        scratch_shapes=[
            pltpu.VMEM((2, 32, CHANNELS, 512), jnp.bfloat16),
            pltpu.VMEM((16, 64, 512), jnp.bfloat16),
        ],
        name="weight_parts",
        compiler_params=pltpu.CompilerParams(vmem_limit_bytes=VMEM_GRANT),
    )(where, *values, *features)


def join_body(kept_ref, received_ref, *outs):
    for flip, out_ref in enumerate(outs):
        total = kept_ref[flip].astype(jnp.float32) + received_ref[flip].astype(jnp.float32)
        out_ref[...] = total.astype(jnp.bfloat16)


def join_cores(kept, received):
    return pl.pallas_call(
        join_body,
        out_shape=(jax.ShapeDtypeStruct((2, 64, 512), jnp.bfloat16),) * 4,
        name="join_cores",
        compiler_params=pltpu.CompilerParams(vmem_limit_bytes=VMEM_GRANT),
    )(kept, received)


def total_body(where_ref, *refs):
    parts, (kept_ref, sent_ref) = refs[:4], refs[4:]
    z = where_ref[3]
    for out_ref, place in ((kept_ref, z), (sent_ref, 1 - z)):
        total = parts[0][place].astype(jnp.float32)
        for part in parts[1:]:
            total = total + part[place].astype(jnp.float32)
        out_ref[...] = (total * ROOT_SCALE).astype(out_ref.dtype)


def weight_total(where, parts):
    return pl.pallas_call(
        total_body,
        out_shape=(
            jax.ShapeDtypeStruct((64, 512), jnp.float32),
            jax.ShapeDtypeStruct((64, 512), jnp.bfloat16),
        ),
        in_specs=[pl.BlockSpec(memory_space=pltpu.SMEM)] + [pl.BlockSpec(memory_space=pltpu.VMEM)] * 4,
        name="weight_total",
        compiler_params=pltpu.CompilerParams(vmem_limit_bytes=VMEM_GRANT),
    )(where, *parts)


def exchange(array):
    return lax.all_to_all(array, "seq", split_axis=0, concat_axis=0, tiled=True)


def ring_step(array, shift):
    return lax.ppermute(array, ("seq", "chan"), along_z(shift))


def shards(layer_input, gate_query, gate_key, value_proj, grad_out, filter_taps):
    tables = [jnp.asarray(table) for table in make_tables()]
    index = lax.axis_index("seq")
    z, y, x, core = index // 32, index // 8 % 4, index // 2 % 4, index % 2
    where = jnp.stack([x, z * 4 + lax.axis_index("chan"), y * 2 + core, z]).astype(jnp.int32)
    pieces = split_features(where, layer_input)
    own = [lax.ppermute(pieces[n], "seq", along_x(n)) for n in range(1, 4)]
    own = jnp.stack([pieces[0]] + own)
    sent = gather_signals(gate_key, value_proj, grad_out, gate_query, filter_taps)
    up, down = ring_step(own, 1), ring_step(own, -1)
    tables = stage(tables)
    signals = exchange(sent)
    up2, down2 = ring_step(up, 1), ring_step(down, -1)
    back_grad, rest, *pieces = convolve(where, signals, tables)
    pieces = pieces[:1] + [lax.ppermute(pieces[n], "seq", across(n)) for n in range(1, 8)]
    up3, down3 = ring_step(up2, 1), ring_step(down2, -1)
    far, far_rest = ring_step(up2[:2], 2), ring_step(down2[2:], -2)
    results = complete(back_grad, rest, tables)
    value = bundle(pieces)
    values = [value] + [lax.ppermute(value, "seq", along_x(n)) for n in range(1, 4)]
    results = exchange(results)
    kept, sent = weight_parts(where, values, (own, up, up2, up3, far, down3, down2, down, far_rest))
    received = lax.ppermute(sent, "seq", across(1))
    parts = join_cores(kept, received)
    parts = [parts[0]] + [lax.ppermute(parts[n], "seq", across(2 * n)) for n in range(1, 4)]
    kept, sent = weight_total(where, parts)
    received = lax.ppermute(sent, "seq", opposite()).astype(jnp.float32)
    grad_query, grad_key, grad_value, grad_filter = finish(results, grad_out, value_proj, gate_key)
    grad_weight = jnp.where(
        z == 0,
        jnp.concatenate([kept, received], axis=1),
        jnp.concatenate([received, kept], axis=1),
    )
    return (grad_query, grad_key, grad_value, grad_filter, grad_weight)


def solution(mesh):
    placed = P("seq", "chan")
    return jax.shard_map(
        shards,
        mesh=mesh,
        in_specs=(placed,) * 6,
        out_specs=(placed,) * 5,
        check_vma=False,
    )
```

```python
import math

import numpy as np

import jax
import jax.numpy as jnp
from jax import lax
from jax.experimental import pallas as pl
from jax.experimental.pallas import tpu as pltpu
from jax.sharding import PartitionSpec as P


BLOCKS = 64
ROWS = 128
CHANNELS = 16
LANES = 3 * CHANNELS
PERIOD = 2 * BLOCKS * ROWS
LAST_SCALE = 1.0 / PERIOD
KEPT = 72
VMEM_GRANT = 12 << 20
ROOT_SCALE = 1.0 / math.sqrt(BLOCKS * ROWS)
SENT = 4 * CHANNELS


def along_x(shift):
    return [(s, s // 8 * 8 + (s // 2 + shift) % 4 * 2 + s % 2) for s in range(64)]


def across(flip):
    pairs = []
    for s in range(64):
        place = (s // 8 % 4 * 2 + s % 2) ^ flip
        pairs.append((s, s // 32 * 32 + place // 2 * 8 + s // 2 % 4 * 2 + place % 2))
    return pairs


def along_z(shift):
    pairs = []
    for flat in range(256):
        s, c = divmod(flat, 4)
        place = (s // 32 * 4 + c + (-shift if s % 2 else shift)) % 8
        pairs.append((flat, (place // 4 * 32 + s % 32) * 4 + place % 4))
    return pairs


def opposite():
    return [(s, (s + 32) % 64) for s in range(64)]


def split_table(table):
    high = table.astype(jnp.bfloat16)
    low = (table - high.astype(np.float64)).astype(jnp.bfloat16)
    return high, low


def make_tables():
    freq = np.arange(KEPT)
    block = np.arange(BLOCKS)
    row = np.arange(ROWS)
    outer = 2.0 * math.pi * (freq[:, None] * block[None, :] % (2 * BLOCKS)) / (2 * BLOCKS)
    first = np.concatenate([np.cos(outer), -np.sin(outer)], axis=0)
    first = np.concatenate(split_table(first), axis=1)
    weight = np.where((freq == 0) | (freq == BLOCKS), 1.0, np.where(freq < BLOCKS, 2.0, 0.0))
    last = np.concatenate([np.cos(outer).T * weight, -np.sin(outer).T * weight], axis=1)
    last = np.concatenate(split_table(last), axis=0)
    twist = 2.0 * math.pi * (freq[:, None] * row[None, :] % PERIOD) / PERIOD
    inner = 2.0 * math.pi * (row[:, None] * row[None, :] % ROWS) / ROWS
    cosine, sine = np.cos(inner), np.sin(inner)
    ahead = np.block([[cosine, -sine], [sine, cosine]])
    return (
        first,
        np.cos(twist).astype(np.float32),
        np.sin(twist).astype(np.float32),
        np.concatenate(split_table(ahead), axis=0),
        np.concatenate(split_table(ahead.T), axis=0),
        last,
    )


def product(left, right):
    return lax.dot_general(left, right, (((1,), (0,)), ((), ())), preferred_element_type=jnp.float32)


WHOLE_GRANT = 60 << 20


def gather_body(key_ref, value_ref, grad_ref, query_ref, taps_ref, sent_ref):
    for part in range(8):
        cols = pl.ds(part * 128, 128)
        key = key_ref[:, cols].astype(jnp.float32)
        mixed = key * value_ref[:, cols].astype(jnp.float32)
        gated = grad_ref[:, cols].astype(jnp.float32) * query_ref[:, cols].astype(jnp.float32)
        for place, signal in enumerate((mixed, taps_ref[:, cols].astype(jnp.float32), gated, key)):
            turned = signal.T.astype(jnp.bfloat16)
            sent_ref[pl.ds(part * 8, 8), pl.ds(place * 16, 16), :] = turned.reshape(8, 16, 128)


def gather_signals(gate_key, value_proj, grad_out, gate_query, filter_taps):
    return pl.pallas_call(
        gather_body,
        out_shape=jax.ShapeDtypeStruct((BLOCKS, SENT, ROWS), jnp.bfloat16),
        name="gather_signals",
        compiler_params=pltpu.CompilerParams(vmem_limit_bytes=WHOLE_GRANT),
    )(gate_key, value_proj, grad_out, gate_query, filter_taps)


def stage_body(*refs):
    half = len(refs) // 2
    for source, target in zip(refs[:half], refs[half:]):
        target[...] = source[...]


def stage(arrays):
    return pl.pallas_call(
        stage_body,
        out_shape=tuple(jax.ShapeDtypeStruct(array.shape, array.dtype) for array in arrays),
        name="stage",
        compiler_params=pltpu.CompilerParams(vmem_limit_bytes=VMEM_GRANT),
    )(*arrays)


def features_body(where_ref, input_ref, *outs):
    for shift, out_ref in enumerate(outs):
        start = (where_ref[0] + shift) % 4 * 128
        for side in range(2):
            block = input_ref[:, pl.ds(pl.multiple_of(side * 512 + start, 128), 128)]
            out_ref[side * 128 : side * 128 + 128, :] = block.astype(jnp.float32).T.astype(jnp.bfloat16)


def split_features(where, layer_input):
    return pl.pallas_call(
        features_body,
        out_shape=(jax.ShapeDtypeStruct((256, ROWS), jnp.bfloat16),) * 4,
        in_specs=[
            pl.BlockSpec(memory_space=pltpu.SMEM),
            pl.BlockSpec(memory_space=pltpu.VMEM),
        ],
        name="split_features",
        compiler_params=pltpu.CompilerParams(vmem_limit_bytes=VMEM_GRANT),
    )(where, layer_input)


UNROLL = 4


def invert(pairs, number, cosine, sine, back_ref, last_ref):
    rowed = product(jnp.concatenate([pairs, pairs], axis=1), back_ref[...])
    bent = []
    for n in range(number):
        real_part = rowed[n * KEPT : n * KEPT + KEPT, :128]
        other_part = rowed[n * KEPT : n * KEPT + KEPT, 128:]
        bent.append(
            jnp.concatenate(
                [
                    real_part * cosine - other_part * sine,
                    real_part * sine + other_part * cosine,
                ],
                axis=0,
            )
        )
    total = product(last_ref[...], jnp.concatenate(bent, axis=1).astype(jnp.bfloat16))
    return total[:BLOCKS] + total[BLOCKS:]


def convolve_body(
    where_ref, signals_ref, first_ref, cos_ref, sin_ref, ahead_ref, back_ref, last_ref,
    out_ref, rest_ref, *refs,
):
    pieces, (wide_in, wide_out, wide_value, sorted_value) = refs[:8], refs[8:]
    wide_in[...] = signals_ref[...].astype(jnp.float32).reshape(BLOCKS * SENT, ROWS)

    def step(index, carry):
        cosine = cos_ref[...]
        sine = sin_ref[...]
        places = [index * UNROLL + inside for inside in range(UNROLL)]
        rows = jnp.concatenate(
            [
                wide_in[pl.ds(place + CHANNELS * s, BLOCKS, stride=SENT), :]
                for place in places
                for s in range(3)
            ],
            axis=1,
        ).astype(jnp.bfloat16)
        outer = product(first_ref[...], jnp.concatenate([rows, rows], axis=0))
        turned = []
        for n in range(3 * UNROLL):
            real_part = outer[:KEPT, n * 128 : n * 128 + 128]
            other_part = outer[KEPT:, n * 128 : n * 128 + 128]
            turned.append(
                jnp.concatenate(
                    [
                        real_part * cosine + other_part * sine,
                        other_part * cosine - real_part * sine,
                    ],
                    axis=1,
                )
            )
        turned = jnp.concatenate(turned, axis=0).astype(jnp.bfloat16)
        spectra = product(jnp.concatenate([turned, turned], axis=1), ahead_ref[...])
        firsts, rest = [], []
        for n in range(UNROLL):
            parts = [
                (spectra[start : start + KEPT, :128], spectra[start : start + KEPT, 128:])
                for start in range(3 * n * KEPT, (3 * n + 3) * KEPT, KEPT)
            ]
            (mixed_real, mixed_other), (taps_real, taps_other), (gated_real, gated_other) = parts
            firsts.append(
                jnp.concatenate(
                    [
                        gated_real * taps_real + gated_other * taps_other,
                        gated_other * taps_real - gated_real * taps_other,
                    ],
                    axis=1,
                )
            )
            rest.append(
                jnp.concatenate(
                    [
                        mixed_real * taps_real - mixed_other * taps_other,
                        mixed_real * taps_other + mixed_other * taps_real,
                    ],
                    axis=1,
                )
            )
            rest.append(
                jnp.concatenate(
                    [
                        gated_real * mixed_real + gated_other * mixed_other,
                        gated_other * mixed_real - gated_real * mixed_other,
                    ],
                    axis=1,
                )
            )
        rest_ref[index] = jnp.concatenate(rest, axis=0).astype(jnp.bfloat16)
        firsts = jnp.concatenate(firsts, axis=0).astype(jnp.bfloat16)
        total = invert(firsts, UNROLL, cosine, sine, back_ref, last_ref)
        for n, place in enumerate(places):
            result = total[:, n * 128 : n * 128 + 128] * LAST_SCALE
            wide_out[pl.ds(place, BLOCKS, stride=CHANNELS), :] = result
            key = wide_in[pl.ds(place + CHANNELS * 3, BLOCKS, stride=SENT), :]
            wide_value[pl.ds(place, BLOCKS, stride=CHANNELS), :] = (
                result.astype(jnp.bfloat16).astype(jnp.float32) * key
            )
        return carry

    lax.fori_loop(0, CHANNELS // UNROLL, step, 0)
    out_ref[...] = wide_out[...].reshape(BLOCKS, CHANNELS, ROWS).astype(jnp.bfloat16)
    for block in range(BLOCKS):
        tile = wide_value[block * CHANNELS : block * CHANNELS + CHANNELS, :].astype(jnp.bfloat16)
        z, y, x, core = block // 32, block // 8 % 4, block // 2 % 4, block % 2
        sorted_value[y * 2 + core, z * 4 + x] = tile
    for flip, piece in enumerate(pieces):
        piece[...] = sorted_value[where_ref[2] ^ flip]


def convolve(where, signals, tables):
    return pl.pallas_call(
        convolve_body,
        out_shape=(
            jax.ShapeDtypeStruct((BLOCKS, CHANNELS, ROWS), jnp.bfloat16),
            jax.ShapeDtypeStruct((CHANNELS // UNROLL, 2 * UNROLL * KEPT, 256), jnp.bfloat16),
        )
        + (jax.ShapeDtypeStruct((8, CHANNELS, ROWS), jnp.bfloat16),) * 8,
        in_specs=[pl.BlockSpec(memory_space=pltpu.SMEM)] + [pl.BlockSpec(memory_space=pltpu.VMEM)] * 7,
        scratch_shapes=[
            pltpu.VMEM((BLOCKS * SENT, ROWS), jnp.float32),
            pltpu.VMEM((BLOCKS * CHANNELS, ROWS), jnp.float32),
            pltpu.VMEM((BLOCKS * CHANNELS, ROWS), jnp.float32),
            pltpu.VMEM((8, 8, CHANNELS, ROWS), jnp.bfloat16),
        ],
        name="convolve",
        compiler_params=pltpu.CompilerParams(vmem_limit_bytes=VMEM_GRANT),
    )(where, signals, *tables)


def complete_body(back_grad_ref, rest_ref, cos_ref, sin_ref, back_ref, last_ref, out_ref, wide_out):
    def step(index, carry):
        cosine = cos_ref[...]
        sine = sin_ref[...]
        total = invert(rest_ref[index], 2 * UNROLL, cosine, sine, back_ref, last_ref)
        for n in range(2 * UNROLL):
            place = index * UNROLL + n // 2
            factor = LAST_SCALE * (ROOT_SCALE if n % 2 else 1.0)
            wide_out[pl.ds(place + CHANNELS * (n % 2), BLOCKS, stride=2 * CHANNELS), :] = (
                total[:, n * 128 : n * 128 + 128] * factor
            )
        return carry

    lax.fori_loop(0, CHANNELS // UNROLL, step, 0)
    wide = wide_out[...].reshape(BLOCKS, 2 * CHANNELS, ROWS).astype(jnp.bfloat16)
    out_ref[:, : 2 * CHANNELS, :] = wide
    out_ref[:, 2 * CHANNELS :, :] = back_grad_ref[...]


def complete(back_grad, rest, tables):
    _, cosine, sine, _, back, last = tables
    return pl.pallas_call(
        complete_body,
        out_shape=jax.ShapeDtypeStruct((BLOCKS, LANES, ROWS), jnp.bfloat16),
        scratch_shapes=[pltpu.VMEM((BLOCKS * 2 * CHANNELS, ROWS), jnp.float32)],
        name="complete",
        compiler_params=pltpu.CompilerParams(vmem_limit_bytes=VMEM_GRANT),
    )(back_grad, rest, cosine, sine, back, last)


def finish_body(back_ref, grad_ref, value_ref, key_ref, query_out, key_out, value_out, filter_out):
    for part in range(8):
        cols = pl.ds(part * 128, 128)

        def turned(place):
            block = back_ref[pl.ds(part * 8, 8), pl.ds(place * 16, 16), :]
            return block.reshape(128, 128).astype(jnp.float32).T

        back = turned(2)
        query_out[:, cols] = (grad_ref[:, cols].astype(jnp.float32) * turned(0)).astype(jnp.bfloat16)
        key_out[:, cols] = (back * value_ref[:, cols].astype(jnp.float32)).astype(jnp.bfloat16)
        value_out[:, cols] = (back * key_ref[:, cols].astype(jnp.float32)).astype(jnp.bfloat16)
        filter_out[:, cols] = turned(1).astype(jnp.bfloat16)


def finish(returned, grad_out, value_proj, gate_key):
    shape = jax.ShapeDtypeStruct(grad_out.shape, jnp.bfloat16)
    return pl.pallas_call(finish_body, out_shape=(shape,) * 4, name="finish", compiler_params=pltpu.CompilerParams(vmem_limit_bytes=VMEM_GRANT))(
        returned, grad_out, value_proj, gate_key
    )


def bundle_body(*refs):
    for n, piece in enumerate(refs[:8]):
        refs[8][n] = piece[...]


def bundle(pieces):
    return pl.pallas_call(
        bundle_body,
        out_shape=jax.ShapeDtypeStruct((8, 8, CHANNELS, ROWS), jnp.bfloat16),
        name="bundle",
        compiler_params=pltpu.CompilerParams(vmem_limit_bytes=VMEM_GRANT),
    )(*pieces)


def weight_body(where_ref, *refs):
    values, features = refs[:4], refs[4:12]
    kept_ref, sent_ref, aligned, pieces = refs[12:]
    x, ring, place = where_ref[0], where_ref[1], where_ref[2]
    turn = 1 - 2 * (place % 2)
    for apart, value_ref in enumerate(values):
        column = (x - apart + 4) % 4
        for flip in range(8):
            origin = place ^ flip
            origin = origin // 2 * 8 + column * 2 + origin % 2
            for z in range(2):
                for back in range(4):
                    aligned[z, origin, :, back * 128 : back * 128 + 128] = value_ref[
                        flip, z * 4 + (x - back + 4) % 4
                    ]
    for apart in range(4):
        total = None
        for half in range(2):
            source = (ring - turn * (apart + 4 * half) + 8) % 8
            rows = features[apart + 4 * half]
            rows = jnp.concatenate([rows[back] for back in range(4)], axis=1)
            term = lax.dot_general(
                rows,
                aligned[source // 4].reshape(512, 512),
                (((1,), (1,)), ((), ())),
                preferred_element_type=jnp.float32,
            )
            total = term if total is None else total + term
        group = (ring - turn * apart + 8) % 4
        for side in range(2):
            for core in range(2):
                target = ((group % 2) * 2 + side) * 2 + core
                start = side * 128 + core * 64
                pieces[target * 2 + group // 2] = total[start : start + 64].astype(jnp.bfloat16)
    side, core = place // 2, place % 2
    for flip in range(4):
        target = (side ^ flip) * 2
        kept_ref[flip] = pieces[pl.ds((target + core) * 2, 2)]
        sent_ref[flip] = pieces[pl.ds((target + 1 - core) * 2, 2)]


def weight_parts(where, values, features):
    return pl.pallas_call(
        weight_body,
        out_shape=(jax.ShapeDtypeStruct((4, 2, 64, 512), jnp.bfloat16),) * 2,
        in_specs=[pl.BlockSpec(memory_space=pltpu.SMEM)]
        + [pl.BlockSpec(memory_space=pltpu.VMEM)] * 12,
        scratch_shapes=[
            pltpu.VMEM((2, 32, CHANNELS, 512), jnp.bfloat16),
            pltpu.VMEM((16, 64, 512), jnp.bfloat16),
        ],
        name="weight_parts",
        compiler_params=pltpu.CompilerParams(vmem_limit_bytes=VMEM_GRANT),
    )(where, *values, *features)


def join_body(kept_ref, received_ref, *outs):
    for flip, out_ref in enumerate(outs):
        total = kept_ref[flip].astype(jnp.float32) + received_ref[flip].astype(jnp.float32)
        out_ref[...] = total.astype(jnp.bfloat16)


def join_cores(kept, received):
    return pl.pallas_call(
        join_body,
        out_shape=(jax.ShapeDtypeStruct((2, 64, 512), jnp.bfloat16),) * 4,
        name="join_cores",
        compiler_params=pltpu.CompilerParams(vmem_limit_bytes=VMEM_GRANT),
    )(kept, received)


def total_body(where_ref, *refs):
    parts, (kept_ref, sent_ref) = refs[:4], refs[4:]
    z = where_ref[3]
    for out_ref, place in ((kept_ref, z), (sent_ref, 1 - z)):
        total = parts[0][place].astype(jnp.float32)
        for part in parts[1:]:
            total = total + part[place].astype(jnp.float32)
        out_ref[...] = (total * ROOT_SCALE).astype(out_ref.dtype)


def weight_total(where, parts):
    return pl.pallas_call(
        total_body,
        out_shape=(
            jax.ShapeDtypeStruct((64, 512), jnp.float32),
            jax.ShapeDtypeStruct((64, 512), jnp.bfloat16),
        ),
        in_specs=[pl.BlockSpec(memory_space=pltpu.SMEM)] + [pl.BlockSpec(memory_space=pltpu.VMEM)] * 4,
        name="weight_total",
        compiler_params=pltpu.CompilerParams(vmem_limit_bytes=VMEM_GRANT),
    )(where, *parts)


def exchange(array):
    return lax.all_to_all(array, "seq", split_axis=0, concat_axis=0, tiled=True)


def ring_step(array, shift):
    return lax.ppermute(array, ("seq", "chan"), along_z(shift))


def shards(layer_input, gate_query, gate_key, value_proj, grad_out, filter_taps):
    tables = [jnp.asarray(table) for table in make_tables()]
    index = lax.axis_index("seq")
    z, y, x, core = index // 32, index // 8 % 4, index // 2 % 4, index % 2
    where = jnp.stack([x, z * 4 + lax.axis_index("chan"), y * 2 + core, z]).astype(jnp.int32)
    pieces = split_features(where, layer_input)
    own = [lax.ppermute(pieces[n], "seq", along_x(n)) for n in range(1, 4)]
    own = jnp.stack([pieces[0]] + own)
    sent = gather_signals(gate_key, value_proj, grad_out, gate_query, filter_taps)
    up, down = ring_step(own, 1), ring_step(own, -1)
    tables = stage(tables)
    signals = exchange(sent)
    up2, down2 = ring_step(up, 1), ring_step(down, -1)
    back_grad, rest, *pieces = convolve(where, signals, tables)
    pieces = pieces[:1] + [lax.ppermute(pieces[n], "seq", across(n)) for n in range(1, 8)]
    up3, down3, far = ring_step(up2, 1), ring_step(down2, -1), ring_step(up2, 2)
    results = complete(back_grad, rest, tables)
    value = bundle(pieces)
    values = [value] + [lax.ppermute(value, "seq", along_x(n)) for n in range(1, 4)]
    results = exchange(results)
    kept, sent = weight_parts(where, values, (own, up, up2, up3, far, down3, down2, down))
    received = lax.ppermute(sent, "seq", across(1))
    parts = join_cores(kept, received)
    parts = [parts[0]] + [lax.ppermute(parts[n], "seq", across(2 * n)) for n in range(1, 4)]
    kept, sent = weight_total(where, parts)
    received = lax.ppermute(sent, "seq", opposite()).astype(jnp.float32)
    grad_query, grad_key, grad_value, grad_filter = finish(results, grad_out, value_proj, gate_key)
    grad_weight = jnp.where(
        z == 0,
        jnp.concatenate([kept, received], axis=1),
        jnp.concatenate([received, kept], axis=1),
    )
    return (grad_query, grad_key, grad_value, grad_filter, grad_weight)


def solution(mesh):
    placed = P("seq", "chan")
    return jax.shard_map(
        shards,
        mesh=mesh,
        in_specs=(placed,) * 6,
        out_specs=(placed,) * 5,
        check_vma=False,
    )
```

```python
import math

import numpy as np

import jax
import jax.numpy as jnp
from jax import lax
from jax.experimental import pallas as pl
from jax.experimental.pallas import tpu as pltpu
from jax.sharding import PartitionSpec as P


BLOCKS = 64
ROWS = 128
CHANNELS = 16
LANES = 3 * CHANNELS
PERIOD = 2 * BLOCKS * ROWS
LAST_SCALE = 1.0 / PERIOD
KEPT = 72
VMEM_GRANT = 12 << 20
ROOT_SCALE = 1.0 / math.sqrt(BLOCKS * ROWS)
SENT = 4 * CHANNELS


def along_x(shift):
    return [(s, s // 8 * 8 + (s // 2 + shift) % 4 * 2 + s % 2) for s in range(64)]


def across(flip):
    pairs = []
    for s in range(64):
        place = (s // 8 % 4 * 2 + s % 2) ^ flip
        pairs.append((s, s // 32 * 32 + place // 2 * 8 + s // 2 % 4 * 2 + place % 2))
    return pairs


def along_z(shift):
    pairs = []
    for flat in range(256):
        s, c = divmod(flat, 4)
        place = (s // 32 * 4 + c + (-shift if s % 2 else shift)) % 8
        pairs.append((flat, (place // 4 * 32 + s % 32) * 4 + place % 4))
    return pairs


def opposite():
    return [(s, (s + 32) % 64) for s in range(64)]


def split_table(table):
    high = table.astype(jnp.bfloat16)
    low = (table - high.astype(np.float64)).astype(jnp.bfloat16)
    return high, low


def make_tables():
    freq = np.arange(KEPT)
    block = np.arange(BLOCKS)
    row = np.arange(ROWS)
    outer = 2.0 * math.pi * (freq[:, None] * block[None, :] % (2 * BLOCKS)) / (2 * BLOCKS)
    first = np.concatenate([np.cos(outer), -np.sin(outer)], axis=0)
    first = np.concatenate(split_table(first), axis=1)
    weight = np.where((freq == 0) | (freq == BLOCKS), 1.0, np.where(freq < BLOCKS, 2.0, 0.0))
    last = np.concatenate([np.cos(outer).T * weight, -np.sin(outer).T * weight], axis=1)
    last = np.concatenate(split_table(last), axis=0)
    twist = 2.0 * math.pi * (freq[:, None] * row[None, :] % PERIOD) / PERIOD
    inner = 2.0 * math.pi * (row[:, None] * row[None, :] % ROWS) / ROWS
    cosine, sine = np.cos(inner), np.sin(inner)
    ahead = np.block([[cosine, -sine], [sine, cosine]])
    return (
        first,
        np.cos(twist).astype(np.float32),
        np.sin(twist).astype(np.float32),
        np.concatenate(split_table(ahead), axis=0),
        np.concatenate(split_table(ahead.T), axis=0),
        last,
    )


def product(left, right):
    return lax.dot_general(left, right, (((1,), (0,)), ((), ())), preferred_element_type=jnp.float32)


WHOLE_GRANT = 60 << 20


def gather_body(key_ref, value_ref, grad_ref, query_ref, taps_ref, sent_ref):
    for part in range(8):
        cols = pl.ds(part * 128, 128)
        key = key_ref[:, cols].astype(jnp.float32)
        mixed = key * value_ref[:, cols].astype(jnp.float32)
        gated = grad_ref[:, cols].astype(jnp.float32) * query_ref[:, cols].astype(jnp.float32)
        for place, signal in enumerate((mixed, taps_ref[:, cols].astype(jnp.float32), gated, key)):
            turned = signal.T.astype(jnp.bfloat16)
            sent_ref[pl.ds(part * 8, 8), pl.ds(place * 16, 16), :] = turned.reshape(8, 16, 128)


def gather_signals(gate_key, value_proj, grad_out, gate_query, filter_taps):
    return pl.pallas_call(
        gather_body,
        out_shape=jax.ShapeDtypeStruct((BLOCKS, SENT, ROWS), jnp.bfloat16),
        name="gather_signals",
        compiler_params=pltpu.CompilerParams(vmem_limit_bytes=WHOLE_GRANT),
    )(gate_key, value_proj, grad_out, gate_query, filter_taps)


def stage_body(*refs):
    half = len(refs) // 2
    for source, target in zip(refs[:half], refs[half:]):
        target[...] = source[...]


def stage(arrays):
    return pl.pallas_call(
        stage_body,
        out_shape=tuple(jax.ShapeDtypeStruct(array.shape, array.dtype) for array in arrays),
        name="stage",
        compiler_params=pltpu.CompilerParams(vmem_limit_bytes=VMEM_GRANT),
    )(*arrays)


def features_body(where_ref, input_ref, *outs):
    for shift, out_ref in enumerate(outs):
        start = (where_ref[0] + shift) % 4 * 128
        for side in range(2):
            block = input_ref[:, pl.ds(pl.multiple_of(side * 512 + start, 128), 128)]
            out_ref[side * 128 : side * 128 + 128, :] = block.astype(jnp.float32).T.astype(jnp.bfloat16)


def split_features(where, layer_input):
    return pl.pallas_call(
        features_body,
        out_shape=(jax.ShapeDtypeStruct((256, ROWS), jnp.bfloat16),) * 4,
        in_specs=[
            pl.BlockSpec(memory_space=pltpu.SMEM),
            pl.BlockSpec(memory_space=pltpu.VMEM),
        ],
        name="split_features",
        compiler_params=pltpu.CompilerParams(vmem_limit_bytes=VMEM_GRANT),
    )(where, layer_input)


UNROLL = 4


def invert(pairs, number, cosine, sine, back_ref, last_ref):
    rowed = product(jnp.concatenate([pairs, pairs], axis=1), back_ref[...])
    bent = []
    for n in range(number):
        real_part = rowed[n * KEPT : n * KEPT + KEPT, :128]
        other_part = rowed[n * KEPT : n * KEPT + KEPT, 128:]
        bent.append(
            jnp.concatenate(
                [
                    real_part * cosine - other_part * sine,
                    real_part * sine + other_part * cosine,
                ],
                axis=0,
            )
        )
    total = product(last_ref[...], jnp.concatenate(bent, axis=1).astype(jnp.bfloat16))
    return total[:BLOCKS] + total[BLOCKS:]


def convolve_body(
    where_ref, signals_ref, first_ref, cos_ref, sin_ref, ahead_ref, back_ref, last_ref,
    out_ref, rest_ref, *refs,
):
    pieces, (wide_in, wide_out, wide_value, sorted_value) = refs[:4], refs[4:]
    wide_in[...] = signals_ref[...].astype(jnp.float32).reshape(BLOCKS * SENT, ROWS)

    def step(index, carry):
        cosine = cos_ref[...]
        sine = sin_ref[...]
        places = [index * UNROLL + inside for inside in range(UNROLL)]
        rows = jnp.concatenate(
            [
                wide_in[pl.ds(place + CHANNELS * s, BLOCKS, stride=SENT), :]
                for place in places
                for s in range(3)
            ],
            axis=1,
        ).astype(jnp.bfloat16)
        outer = product(first_ref[...], jnp.concatenate([rows, rows], axis=0))
        turned = []
        for n in range(3 * UNROLL):
            real_part = outer[:KEPT, n * 128 : n * 128 + 128]
            other_part = outer[KEPT:, n * 128 : n * 128 + 128]
            turned.append(
                jnp.concatenate(
                    [
                        real_part * cosine + other_part * sine,
                        other_part * cosine - real_part * sine,
                    ],
                    axis=1,
                )
            )
        turned = jnp.concatenate(turned, axis=0).astype(jnp.bfloat16)
        spectra = product(jnp.concatenate([turned, turned], axis=1), ahead_ref[...])
        firsts, rest = [], []
        for n in range(UNROLL):
            parts = [
                (spectra[start : start + KEPT, :128], spectra[start : start + KEPT, 128:])
                for start in range(3 * n * KEPT, (3 * n + 3) * KEPT, KEPT)
            ]
            (mixed_real, mixed_other), (taps_real, taps_other), (gated_real, gated_other) = parts
            firsts.append(
                jnp.concatenate(
                    [
                        gated_real * taps_real + gated_other * taps_other,
                        gated_other * taps_real - gated_real * taps_other,
                    ],
                    axis=1,
                )
            )
            rest.append(
                jnp.concatenate(
                    [
                        mixed_real * taps_real - mixed_other * taps_other,
                        mixed_real * taps_other + mixed_other * taps_real,
                    ],
                    axis=1,
                )
            )
            rest.append(
                jnp.concatenate(
                    [
                        gated_real * mixed_real + gated_other * mixed_other,
                        gated_other * mixed_real - gated_real * mixed_other,
                    ],
                    axis=1,
                )
            )
        rest_ref[index] = jnp.concatenate(rest, axis=0).astype(jnp.bfloat16)
        firsts = jnp.concatenate(firsts, axis=0).astype(jnp.bfloat16)
        total = invert(firsts, UNROLL, cosine, sine, back_ref, last_ref)
        for n, place in enumerate(places):
            result = total[:, n * 128 : n * 128 + 128] * LAST_SCALE
            wide_out[pl.ds(place, BLOCKS, stride=CHANNELS), :] = result
            key = wide_in[pl.ds(place + CHANNELS * 3, BLOCKS, stride=SENT), :]
            wide_value[pl.ds(place, BLOCKS, stride=CHANNELS), :] = (
                result.astype(jnp.bfloat16).astype(jnp.float32) * key
            )
        return carry

    lax.fori_loop(0, CHANNELS // UNROLL, step, 0)
    out_ref[...] = wide_out[...].reshape(BLOCKS, CHANNELS, ROWS).astype(jnp.bfloat16)
    for block in range(BLOCKS):
        tile = wide_value[block * CHANNELS : block * CHANNELS + CHANNELS, :].astype(jnp.bfloat16)
        z, y, x, core = block // 32, block // 8 % 4, block // 2 % 4, block % 2
        sorted_value[y * 2 + core, z * 4 + x] = tile
    for flip, piece in enumerate(pieces):
        for other in range(2):
            piece[other] = sorted_value[where_ref[2] ^ (2 * flip + other)]


def convolve(where, signals, tables):
    return pl.pallas_call(
        convolve_body,
        out_shape=(
            jax.ShapeDtypeStruct((BLOCKS, CHANNELS, ROWS), jnp.bfloat16),
            jax.ShapeDtypeStruct((CHANNELS // UNROLL, 2 * UNROLL * KEPT, 256), jnp.bfloat16),
        )
        + (jax.ShapeDtypeStruct((2, 8, CHANNELS, ROWS), jnp.bfloat16),) * 4,
        in_specs=[pl.BlockSpec(memory_space=pltpu.SMEM)] + [pl.BlockSpec(memory_space=pltpu.VMEM)] * 7,
        scratch_shapes=[
            pltpu.VMEM((BLOCKS * SENT, ROWS), jnp.float32),
            pltpu.VMEM((BLOCKS * CHANNELS, ROWS), jnp.float32),
            pltpu.VMEM((BLOCKS * CHANNELS, ROWS), jnp.float32),
            pltpu.VMEM((8, 8, CHANNELS, ROWS), jnp.bfloat16),
        ],
        name="convolve",
        compiler_params=pltpu.CompilerParams(vmem_limit_bytes=VMEM_GRANT),
    )(where, signals, *tables)


def complete_body(back_grad_ref, rest_ref, cos_ref, sin_ref, back_ref, last_ref, out_ref, wide_out):
    def step(index, carry):
        cosine = cos_ref[...]
        sine = sin_ref[...]
        total = invert(rest_ref[index], 2 * UNROLL, cosine, sine, back_ref, last_ref)
        for n in range(2 * UNROLL):
            place = index * UNROLL + n // 2
            factor = LAST_SCALE * (ROOT_SCALE if n % 2 else 1.0)
            wide_out[pl.ds(place + CHANNELS * (n % 2), BLOCKS, stride=2 * CHANNELS), :] = (
                total[:, n * 128 : n * 128 + 128] * factor
            )
        return carry

    lax.fori_loop(0, CHANNELS // UNROLL, step, 0)
    wide = wide_out[...].reshape(BLOCKS, 2 * CHANNELS, ROWS).astype(jnp.bfloat16)
    out_ref[:, : 2 * CHANNELS, :] = wide
    out_ref[:, 2 * CHANNELS :, :] = back_grad_ref[...]


def complete(back_grad, rest, tables):
    _, cosine, sine, _, back, last = tables
    return pl.pallas_call(
        complete_body,
        out_shape=jax.ShapeDtypeStruct((BLOCKS, LANES, ROWS), jnp.bfloat16),
        scratch_shapes=[pltpu.VMEM((BLOCKS * 2 * CHANNELS, ROWS), jnp.float32)],
        name="complete",
        compiler_params=pltpu.CompilerParams(vmem_limit_bytes=VMEM_GRANT),
    )(back_grad, rest, cosine, sine, back, last)


def finish_body(back_ref, grad_ref, value_ref, key_ref, query_out, key_out, value_out, filter_out):
    for part in range(8):
        cols = pl.ds(part * 128, 128)

        def turned(place):
            block = back_ref[pl.ds(part * 8, 8), pl.ds(place * 16, 16), :]
            return block.reshape(128, 128).astype(jnp.float32).T

        back = turned(2)
        query_out[:, cols] = (grad_ref[:, cols].astype(jnp.float32) * turned(0)).astype(jnp.bfloat16)
        key_out[:, cols] = (back * value_ref[:, cols].astype(jnp.float32)).astype(jnp.bfloat16)
        value_out[:, cols] = (back * key_ref[:, cols].astype(jnp.float32)).astype(jnp.bfloat16)
        filter_out[:, cols] = turned(1).astype(jnp.bfloat16)


def finish(returned, grad_out, value_proj, gate_key):
    shape = jax.ShapeDtypeStruct(grad_out.shape, jnp.bfloat16)
    return pl.pallas_call(finish_body, out_shape=(shape,) * 4, name="finish", compiler_params=pltpu.CompilerParams(vmem_limit_bytes=VMEM_GRANT))(
        returned, grad_out, value_proj, gate_key
    )


def sort_body(*refs):
    pieces, (kept_ref, sent_ref) = refs[:4], refs[4:]
    for n, piece in enumerate(pieces):
        kept_ref[n] = piece[0]
        sent_ref[n] = piece[1]


def sort_cores(pieces):
    return pl.pallas_call(
        sort_body,
        out_shape=(jax.ShapeDtypeStruct((4, 8, CHANNELS, ROWS), jnp.bfloat16),) * 2,
        name="sort_cores",
        compiler_params=pltpu.CompilerParams(vmem_limit_bytes=VMEM_GRANT),
    )(*pieces)


def bundle_body(kept_ref, received_ref, out_ref):
    for n in range(4):
        out_ref[2 * n] = kept_ref[n]
        out_ref[2 * n + 1] = received_ref[n]


def bundle(kept, received):
    return pl.pallas_call(
        bundle_body,
        out_shape=jax.ShapeDtypeStruct((8, 8, CHANNELS, ROWS), jnp.bfloat16),
        name="bundle",
        compiler_params=pltpu.CompilerParams(vmem_limit_bytes=VMEM_GRANT),
    )(kept, received)


def weight_body(where_ref, *refs):
    values, features = refs[:4], refs[4:12]
    kept_ref, sent_ref, aligned, pieces = refs[12:]
    x, ring, place = where_ref[0], where_ref[1], where_ref[2]
    turn = 1 - 2 * (place % 2)
    for apart, value_ref in enumerate(values):
        column = (x - apart + 4) % 4
        for flip in range(8):
            origin = place ^ flip
            origin = origin // 2 * 8 + column * 2 + origin % 2
            for z in range(2):
                for back in range(4):
                    aligned[z, origin, :, back * 128 : back * 128 + 128] = value_ref[
                        flip, z * 4 + (x - back + 4) % 4
                    ]
    for apart in range(4):
        total = None
        for half in range(2):
            source = (ring - turn * (apart + 4 * half) + 8) % 8
            rows = features[apart + 4 * half]
            rows = jnp.concatenate([rows[back] for back in range(4)], axis=1)
            term = lax.dot_general(
                rows,
                aligned[source // 4].reshape(512, 512),
                (((1,), (1,)), ((), ())),
                preferred_element_type=jnp.float32,
            )
            total = term if total is None else total + term
        group = (ring - turn * apart + 8) % 4
        for side in range(2):
            for core in range(2):
                target = ((group % 2) * 2 + side) * 2 + core
                start = side * 128 + core * 64
                pieces[target * 2 + group // 2] = total[start : start + 64].astype(jnp.bfloat16)
    side, core = place // 2, place % 2
    for flip in range(4):
        target = (side ^ flip) * 2
        kept_ref[flip] = pieces[pl.ds((target + core) * 2, 2)]
        sent_ref[flip] = pieces[pl.ds((target + 1 - core) * 2, 2)]


def weight_parts(where, values, features):
    return pl.pallas_call(
        weight_body,
        out_shape=(jax.ShapeDtypeStruct((4, 2, 64, 512), jnp.bfloat16),) * 2,
        in_specs=[pl.BlockSpec(memory_space=pltpu.SMEM)]
        + [pl.BlockSpec(memory_space=pltpu.VMEM)] * 12,
        scratch_shapes=[
            pltpu.VMEM((2, 32, CHANNELS, 512), jnp.bfloat16),
            pltpu.VMEM((16, 64, 512), jnp.bfloat16),
        ],
        name="weight_parts",
        compiler_params=pltpu.CompilerParams(vmem_limit_bytes=VMEM_GRANT),
    )(where, *values, *features)


def join_body(kept_ref, received_ref, *outs):
    for flip, out_ref in enumerate(outs):
        total = kept_ref[flip].astype(jnp.float32) + received_ref[flip].astype(jnp.float32)
        out_ref[...] = total.astype(jnp.bfloat16)


def join_cores(kept, received):
    return pl.pallas_call(
        join_body,
        out_shape=(jax.ShapeDtypeStruct((2, 64, 512), jnp.bfloat16),) * 4,
        name="join_cores",
        compiler_params=pltpu.CompilerParams(vmem_limit_bytes=VMEM_GRANT),
    )(kept, received)


def total_body(where_ref, *refs):
    parts, (kept_ref, sent_ref) = refs[:4], refs[4:]
    z = where_ref[3]
    for out_ref, place in ((kept_ref, z), (sent_ref, 1 - z)):
        total = parts[0][place].astype(jnp.float32)
        for part in parts[1:]:
            total = total + part[place].astype(jnp.float32)
        out_ref[...] = (total * ROOT_SCALE).astype(out_ref.dtype)


def weight_total(where, parts):
    return pl.pallas_call(
        total_body,
        out_shape=(
            jax.ShapeDtypeStruct((64, 512), jnp.float32),
            jax.ShapeDtypeStruct((64, 512), jnp.bfloat16),
        ),
        in_specs=[pl.BlockSpec(memory_space=pltpu.SMEM)] + [pl.BlockSpec(memory_space=pltpu.VMEM)] * 4,
        name="weight_total",
        compiler_params=pltpu.CompilerParams(vmem_limit_bytes=VMEM_GRANT),
    )(where, *parts)


def exchange(array):
    return lax.all_to_all(array, "seq", split_axis=0, concat_axis=0, tiled=True)


def ring_step(array, shift):
    return lax.ppermute(array, ("seq", "chan"), along_z(shift))


def shards(layer_input, gate_query, gate_key, value_proj, grad_out, filter_taps):
    tables = [jnp.asarray(table) for table in make_tables()]
    index = lax.axis_index("seq")
    z, y, x, core = index // 32, index // 8 % 4, index // 2 % 4, index % 2
    where = jnp.stack([x, z * 4 + lax.axis_index("chan"), y * 2 + core, z]).astype(jnp.int32)
    pieces = split_features(where, layer_input)
    own = [lax.ppermute(pieces[n], "seq", along_x(n)) for n in range(1, 4)]
    own = jnp.stack([pieces[0]] + own)
    sent = gather_signals(gate_key, value_proj, grad_out, gate_query, filter_taps)
    up, down = ring_step(own, 1), ring_step(own, -1)
    tables = stage(tables)
    signals = exchange(sent)
    up2, down2 = ring_step(up, 1), ring_step(down, -1)
    back_grad, rest, *pieces = convolve(where, signals, tables)
    pieces = pieces[:1] + [lax.ppermute(pieces[n], "seq", across(2 * n)) for n in range(1, 4)]
    kept, sent = sort_cores(pieces)
    received = lax.ppermute(sent, "seq", across(1))
    up3, down3, far = ring_step(up2, 1), ring_step(down2, -1), ring_step(up2, 2)
    results = complete(back_grad, rest, tables)
    value = bundle(kept, received)
    values = [value] + [lax.ppermute(value, "seq", along_x(n)) for n in range(1, 4)]
    results = exchange(results)
    kept, sent = weight_parts(where, values, (own, up, up2, up3, far, down3, down2, down))
    received = lax.ppermute(sent, "seq", across(1))
    parts = join_cores(kept, received)
    parts = [parts[0]] + [lax.ppermute(parts[n], "seq", across(2 * n)) for n in range(1, 4)]
    kept, sent = weight_total(where, parts)
    received = lax.ppermute(sent, "seq", opposite()).astype(jnp.float32)
    grad_query, grad_key, grad_value, grad_filter = finish(results, grad_out, value_proj, gate_key)
    grad_weight = jnp.where(
        z == 0,
        jnp.concatenate([kept, received], axis=1),
        jnp.concatenate([received, kept], axis=1),
    )
    return (grad_query, grad_key, grad_value, grad_filter, grad_weight)


def solution(mesh):
    placed = P("seq", "chan")
    return jax.shard_map(
        shards,
        mesh=mesh,
        in_specs=(placed,) * 6,
        out_specs=(placed,) * 5,
        check_vma=False,
    )
```

```python
import math

import numpy as np

import jax
import jax.numpy as jnp
from jax import lax
from jax.experimental import pallas as pl
from jax.experimental.pallas import tpu as pltpu
from jax.sharding import PartitionSpec as P


BLOCKS = 64
ROWS = 128
CHANNELS = 16
LANES = 3 * CHANNELS
PERIOD = 2 * BLOCKS * ROWS
LAST_SCALE = 1.0 / PERIOD
KEPT = 72
VMEM_GRANT = 12 << 20
ROOT_SCALE = 1.0 / math.sqrt(BLOCKS * ROWS)
SENT = 4 * CHANNELS


def along_x(shift):
    return [(s, s // 8 * 8 + (s // 2 + shift) % 4 * 2 + s % 2) for s in range(64)]


def across(flip):
    pairs = []
    for s in range(64):
        place = (s // 8 % 4 * 2 + s % 2) ^ flip
        pairs.append((s, s // 32 * 32 + place // 2 * 8 + s // 2 % 4 * 2 + place % 2))
    return pairs


def along_z(shift):
    pairs = []
    for flat in range(256):
        s, c = divmod(flat, 4)
        place = (s // 32 * 4 + c + (-shift if s % 2 else shift)) % 8
        pairs.append((flat, (place // 4 * 32 + s % 32) * 4 + place % 4))
    return pairs


def opposite():
    return [(s, (s + 32) % 64) for s in range(64)]


def split_table(table):
    high = table.astype(jnp.bfloat16)
    low = (table - high.astype(np.float64)).astype(jnp.bfloat16)
    return high, low


def make_tables():
    freq = np.arange(KEPT)
    block = np.arange(BLOCKS)
    row = np.arange(ROWS)
    outer = 2.0 * math.pi * (freq[:, None] * block[None, :] % (2 * BLOCKS)) / (2 * BLOCKS)
    first = np.concatenate([np.cos(outer), -np.sin(outer)], axis=0)
    first = np.concatenate(split_table(first), axis=1)
    weight = np.where((freq == 0) | (freq == BLOCKS), 1.0, np.where(freq < BLOCKS, 2.0, 0.0))
    last = np.concatenate([np.cos(outer).T * weight, -np.sin(outer).T * weight], axis=1)
    last = np.concatenate(split_table(last), axis=0)
    twist = 2.0 * math.pi * (freq[:, None] * row[None, :] % PERIOD) / PERIOD
    inner = 2.0 * math.pi * (row[:, None] * row[None, :] % ROWS) / ROWS
    cosine, sine = np.cos(inner), np.sin(inner)
    ahead = np.block([[cosine, -sine], [sine, cosine]])
    return (
        first,
        np.cos(twist).astype(np.float32),
        np.sin(twist).astype(np.float32),
        np.concatenate(split_table(ahead), axis=0),
        np.concatenate(split_table(ahead.T), axis=0),
        last,
    )


def product(left, right):
    return lax.dot_general(left, right, (((1,), (0,)), ((), ())), preferred_element_type=jnp.float32)


WHOLE_GRANT = 60 << 20


def gather_body(key_ref, value_ref, grad_ref, query_ref, taps_ref, sent_ref):
    for part in range(8):
        cols = pl.ds(part * 128, 128)
        key = key_ref[:, cols].astype(jnp.float32)
        mixed = key * value_ref[:, cols].astype(jnp.float32)
        gated = grad_ref[:, cols].astype(jnp.float32) * query_ref[:, cols].astype(jnp.float32)
        for place, signal in enumerate((mixed, taps_ref[:, cols].astype(jnp.float32), gated, key)):
            turned = signal.T.astype(jnp.bfloat16)
            sent_ref[pl.ds(part * 8, 8), pl.ds(place * 16, 16), :] = turned.reshape(8, 16, 128)


def gather_signals(gate_key, value_proj, grad_out, gate_query, filter_taps):
    return pl.pallas_call(
        gather_body,
        out_shape=jax.ShapeDtypeStruct((BLOCKS, SENT, ROWS), jnp.bfloat16),
        name="gather_signals",
        compiler_params=pltpu.CompilerParams(vmem_limit_bytes=WHOLE_GRANT),
    )(gate_key, value_proj, grad_out, gate_query, filter_taps)


def stage_body(*refs):
    half = len(refs) // 2
    for source, target in zip(refs[:half], refs[half:]):
        target[...] = source[...]


def stage(arrays):
    return pl.pallas_call(
        stage_body,
        out_shape=tuple(jax.ShapeDtypeStruct(array.shape, array.dtype) for array in arrays),
        name="stage",
        compiler_params=pltpu.CompilerParams(vmem_limit_bytes=VMEM_GRANT),
    )(*arrays)


def features_body(where_ref, input_ref, *outs):
    for shift, out_ref in enumerate(outs):
        start = (where_ref[0] + shift) % 4 * 128
        for side in range(2):
            block = input_ref[:, pl.ds(pl.multiple_of(side * 512 + start, 128), 128)]
            out_ref[side * 128 : side * 128 + 128, :] = block.astype(jnp.float32).T.astype(jnp.bfloat16)


def split_features(where, layer_input):
    return pl.pallas_call(
        features_body,
        out_shape=(jax.ShapeDtypeStruct((256, ROWS), jnp.bfloat16),) * 4,
        in_specs=[
            pl.BlockSpec(memory_space=pltpu.SMEM),
            pl.BlockSpec(memory_space=pltpu.VMEM),
        ],
        name="split_features",
        compiler_params=pltpu.CompilerParams(vmem_limit_bytes=VMEM_GRANT),
    )(where, layer_input)


UNROLL = 8


def invert(pairs, number, cosine, sine, back_ref, last_ref):
    rowed = product(jnp.concatenate([pairs, pairs], axis=1), back_ref[...])
    bent = []
    for n in range(number):
        real_part = rowed[n * KEPT : n * KEPT + KEPT, :128]
        other_part = rowed[n * KEPT : n * KEPT + KEPT, 128:]
        bent.append(
            jnp.concatenate(
                [
                    real_part * cosine - other_part * sine,
                    real_part * sine + other_part * cosine,
                ],
                axis=0,
            )
        )
    total = product(last_ref[...], jnp.concatenate(bent, axis=1).astype(jnp.bfloat16))
    return total[:BLOCKS] + total[BLOCKS:]


def convolve_body(
    where_ref, signals_ref, first_ref, cos_ref, sin_ref, ahead_ref, back_ref, last_ref,
    out_ref, rest_ref, *refs,
):
    pieces, (wide_in, wide_out, wide_value, sorted_value) = refs[:4], refs[4:]
    wide_in[...] = signals_ref[...].astype(jnp.float32).reshape(BLOCKS * SENT, ROWS)

    def step(index, carry):
        cosine = cos_ref[...]
        sine = sin_ref[...]
        places = [index * UNROLL + inside for inside in range(UNROLL)]
        rows = jnp.concatenate(
            [
                wide_in[pl.ds(place + CHANNELS * s, BLOCKS, stride=SENT), :]
                for place in places
                for s in range(3)
            ],
            axis=1,
        ).astype(jnp.bfloat16)
        outer = product(first_ref[...], jnp.concatenate([rows, rows], axis=0))
        turned = []
        for n in range(3 * UNROLL):
            real_part = outer[:KEPT, n * 128 : n * 128 + 128]
            other_part = outer[KEPT:, n * 128 : n * 128 + 128]
            turned.append(
                jnp.concatenate(
                    [
                        real_part * cosine + other_part * sine,
                        other_part * cosine - real_part * sine,
                    ],
                    axis=1,
                )
            )
        turned = jnp.concatenate(turned, axis=0).astype(jnp.bfloat16)
        spectra = product(jnp.concatenate([turned, turned], axis=1), ahead_ref[...])
        firsts, rest = [], []
        for n in range(UNROLL):
            parts = [
                (spectra[start : start + KEPT, :128], spectra[start : start + KEPT, 128:])
                for start in range(3 * n * KEPT, (3 * n + 3) * KEPT, KEPT)
            ]
            (mixed_real, mixed_other), (taps_real, taps_other), (gated_real, gated_other) = parts
            firsts.append(
                jnp.concatenate(
                    [
                        gated_real * taps_real + gated_other * taps_other,
                        gated_other * taps_real - gated_real * taps_other,
                    ],
                    axis=1,
                )
            )
            rest.append(
                jnp.concatenate(
                    [
                        mixed_real * taps_real - mixed_other * taps_other,
                        mixed_real * taps_other + mixed_other * taps_real,
                    ],
                    axis=1,
                )
            )
            rest.append(
                jnp.concatenate(
                    [
                        gated_real * mixed_real + gated_other * mixed_other,
                        gated_other * mixed_real - gated_real * mixed_other,
                    ],
                    axis=1,
                )
            )
        rest_ref[index] = jnp.concatenate(rest, axis=0).astype(jnp.bfloat16)
        firsts = jnp.concatenate(firsts, axis=0).astype(jnp.bfloat16)
        total = invert(firsts, UNROLL, cosine, sine, back_ref, last_ref)
        for n, place in enumerate(places):
            result = total[:, n * 128 : n * 128 + 128] * LAST_SCALE
            wide_out[pl.ds(place, BLOCKS, stride=CHANNELS), :] = result
            key = wide_in[pl.ds(place + CHANNELS * 3, BLOCKS, stride=SENT), :]
            wide_value[pl.ds(place, BLOCKS, stride=CHANNELS), :] = (
                result.astype(jnp.bfloat16).astype(jnp.float32) * key
            )
        return carry

    lax.fori_loop(0, CHANNELS // UNROLL, step, 0)
    out_ref[...] = wide_out[...].reshape(BLOCKS, CHANNELS, ROWS).astype(jnp.bfloat16)
    for block in range(BLOCKS):
        tile = wide_value[block * CHANNELS : block * CHANNELS + CHANNELS, :].astype(jnp.bfloat16)
        z, y, x, core = block // 32, block // 8 % 4, block // 2 % 4, block % 2
        sorted_value[y * 2 + core, z * 4 + x] = tile
    for flip, piece in enumerate(pieces):
        for other in range(2):
            piece[other] = sorted_value[where_ref[2] ^ (2 * flip + other)]


def convolve(where, signals, tables):
    return pl.pallas_call(
        convolve_body,
        out_shape=(
            jax.ShapeDtypeStruct((BLOCKS, CHANNELS, ROWS), jnp.bfloat16),
            jax.ShapeDtypeStruct((CHANNELS // UNROLL, 2 * UNROLL * KEPT, 256), jnp.bfloat16),
        )
        + (jax.ShapeDtypeStruct((2, 8, CHANNELS, ROWS), jnp.bfloat16),) * 4,
        in_specs=[pl.BlockSpec(memory_space=pltpu.SMEM)] + [pl.BlockSpec(memory_space=pltpu.VMEM)] * 7,
        scratch_shapes=[
            pltpu.VMEM((BLOCKS * SENT, ROWS), jnp.float32),
            pltpu.VMEM((BLOCKS * CHANNELS, ROWS), jnp.float32),
            pltpu.VMEM((BLOCKS * CHANNELS, ROWS), jnp.float32),
            pltpu.VMEM((8, 8, CHANNELS, ROWS), jnp.bfloat16),
        ],
        name="convolve",
        compiler_params=pltpu.CompilerParams(vmem_limit_bytes=VMEM_GRANT),
    )(where, signals, *tables)


def complete_body(back_grad_ref, rest_ref, cos_ref, sin_ref, back_ref, last_ref, out_ref, wide_out):
    def step(index, carry):
        cosine = cos_ref[...]
        sine = sin_ref[...]
        total = invert(rest_ref[index], 2 * UNROLL, cosine, sine, back_ref, last_ref)
        for n in range(2 * UNROLL):
            place = index * UNROLL + n // 2
            factor = LAST_SCALE * (ROOT_SCALE if n % 2 else 1.0)
            wide_out[pl.ds(place + CHANNELS * (n % 2), BLOCKS, stride=2 * CHANNELS), :] = (
                total[:, n * 128 : n * 128 + 128] * factor
            )
        return carry

    lax.fori_loop(0, CHANNELS // UNROLL, step, 0)
    wide = wide_out[...].reshape(BLOCKS, 2 * CHANNELS, ROWS).astype(jnp.bfloat16)
    out_ref[:, : 2 * CHANNELS, :] = wide
    out_ref[:, 2 * CHANNELS :, :] = back_grad_ref[...]


def complete(back_grad, rest, tables):
    _, cosine, sine, _, back, last = tables
    return pl.pallas_call(
        complete_body,
        out_shape=jax.ShapeDtypeStruct((BLOCKS, LANES, ROWS), jnp.bfloat16),
        scratch_shapes=[pltpu.VMEM((BLOCKS * 2 * CHANNELS, ROWS), jnp.float32)],
        name="complete",
        compiler_params=pltpu.CompilerParams(vmem_limit_bytes=VMEM_GRANT),
    )(back_grad, rest, cosine, sine, back, last)


def finish_body(back_ref, grad_ref, value_ref, key_ref, query_out, key_out, value_out, filter_out):
    for part in range(8):
        cols = pl.ds(part * 128, 128)

        def turned(place):
            block = back_ref[pl.ds(part * 8, 8), pl.ds(place * 16, 16), :]
            return block.reshape(128, 128).astype(jnp.float32).T

        back = turned(2)
        query_out[:, cols] = (grad_ref[:, cols].astype(jnp.float32) * turned(0)).astype(jnp.bfloat16)
        key_out[:, cols] = (back * value_ref[:, cols].astype(jnp.float32)).astype(jnp.bfloat16)
        value_out[:, cols] = (back * key_ref[:, cols].astype(jnp.float32)).astype(jnp.bfloat16)
        filter_out[:, cols] = turned(1).astype(jnp.bfloat16)


def finish(returned, grad_out, value_proj, gate_key):
    shape = jax.ShapeDtypeStruct(grad_out.shape, jnp.bfloat16)
    return pl.pallas_call(finish_body, out_shape=(shape,) * 4, name="finish", compiler_params=pltpu.CompilerParams(vmem_limit_bytes=VMEM_GRANT))(
        returned, grad_out, value_proj, gate_key
    )


def sort_body(*refs):
    pieces, (kept_ref, sent_ref) = refs[:4], refs[4:]
    for n, piece in enumerate(pieces):
        kept_ref[n] = piece[0]
        sent_ref[n] = piece[1]


def sort_cores(pieces):
    return pl.pallas_call(
        sort_body,
        out_shape=(jax.ShapeDtypeStruct((4, 8, CHANNELS, ROWS), jnp.bfloat16),) * 2,
        name="sort_cores",
        compiler_params=pltpu.CompilerParams(vmem_limit_bytes=VMEM_GRANT),
    )(*pieces)


def bundle_body(kept_ref, received_ref, out_ref):
    for n in range(4):
        out_ref[2 * n] = kept_ref[n]
        out_ref[2 * n + 1] = received_ref[n]


def bundle(kept, received):
    return pl.pallas_call(
        bundle_body,
        out_shape=jax.ShapeDtypeStruct((8, 8, CHANNELS, ROWS), jnp.bfloat16),
        name="bundle",
        compiler_params=pltpu.CompilerParams(vmem_limit_bytes=VMEM_GRANT),
    )(kept, received)


def weight_body(where_ref, *refs):
    values, features = refs[:4], refs[4:12]
    kept_ref, sent_ref, aligned, pieces = refs[12:]
    x, ring, place = where_ref[0], where_ref[1], where_ref[2]
    turn = 1 - 2 * (place % 2)
    for apart, value_ref in enumerate(values):
        column = (x - apart + 4) % 4
        for flip in range(8):
            origin = place ^ flip
            origin = origin // 2 * 8 + column * 2 + origin % 2
            for z in range(2):
                for back in range(4):
                    aligned[z, origin, :, back * 128 : back * 128 + 128] = value_ref[
                        flip, z * 4 + (x - back + 4) % 4
                    ]
    for apart in range(4):
        total = None
        for half in range(2):
            source = (ring - turn * (apart + 4 * half) + 8) % 8
            rows = features[apart + 4 * half]
            rows = jnp.concatenate([rows[back] for back in range(4)], axis=1)
            term = lax.dot_general(
                rows,
                aligned[source // 4].reshape(512, 512),
                (((1,), (1,)), ((), ())),
                preferred_element_type=jnp.float32,
            )
            total = term if total is None else total + term
        group = (ring - turn * apart + 8) % 4
        for side in range(2):
            for core in range(2):
                target = ((group % 2) * 2 + side) * 2 + core
                start = side * 128 + core * 64
                pieces[target * 2 + group // 2] = total[start : start + 64].astype(jnp.bfloat16)
    side, core = place // 2, place % 2
    for flip in range(4):
        target = (side ^ flip) * 2
        kept_ref[flip] = pieces[pl.ds((target + core) * 2, 2)]
        sent_ref[flip] = pieces[pl.ds((target + 1 - core) * 2, 2)]


def weight_parts(where, values, features):
    return pl.pallas_call(
        weight_body,
        out_shape=(jax.ShapeDtypeStruct((4, 2, 64, 512), jnp.bfloat16),) * 2,
        in_specs=[pl.BlockSpec(memory_space=pltpu.SMEM)]
        + [pl.BlockSpec(memory_space=pltpu.VMEM)] * 12,
        scratch_shapes=[
            pltpu.VMEM((2, 32, CHANNELS, 512), jnp.bfloat16),
            pltpu.VMEM((16, 64, 512), jnp.bfloat16),
        ],
        name="weight_parts",
        compiler_params=pltpu.CompilerParams(vmem_limit_bytes=VMEM_GRANT),
    )(where, *values, *features)


def join_body(kept_ref, received_ref, *outs):
    for flip, out_ref in enumerate(outs):
        total = kept_ref[flip].astype(jnp.float32) + received_ref[flip].astype(jnp.float32)
        out_ref[...] = total.astype(jnp.bfloat16)


def join_cores(kept, received):
    return pl.pallas_call(
        join_body,
        out_shape=(jax.ShapeDtypeStruct((2, 64, 512), jnp.bfloat16),) * 4,
        name="join_cores",
        compiler_params=pltpu.CompilerParams(vmem_limit_bytes=VMEM_GRANT),
    )(kept, received)


def total_body(where_ref, *refs):
    parts, (kept_ref, sent_ref) = refs[:4], refs[4:]
    z = where_ref[3]
    for out_ref, place in ((kept_ref, z), (sent_ref, 1 - z)):
        total = parts[0][place].astype(jnp.float32)
        for part in parts[1:]:
            total = total + part[place].astype(jnp.float32)
        out_ref[...] = (total * ROOT_SCALE).astype(out_ref.dtype)


def weight_total(where, parts):
    return pl.pallas_call(
        total_body,
        out_shape=(
            jax.ShapeDtypeStruct((64, 512), jnp.float32),
            jax.ShapeDtypeStruct((64, 512), jnp.bfloat16),
        ),
        in_specs=[pl.BlockSpec(memory_space=pltpu.SMEM)] + [pl.BlockSpec(memory_space=pltpu.VMEM)] * 4,
        name="weight_total",
        compiler_params=pltpu.CompilerParams(vmem_limit_bytes=VMEM_GRANT),
    )(where, *parts)


def exchange(array):
    return lax.all_to_all(array, "seq", split_axis=0, concat_axis=0, tiled=True)


def ring_step(array, shift):
    return lax.ppermute(array, ("seq", "chan"), along_z(shift))


def shards(layer_input, gate_query, gate_key, value_proj, grad_out, filter_taps):
    tables = [jnp.asarray(table) for table in make_tables()]
    index = lax.axis_index("seq")
    z, y, x, core = index // 32, index // 8 % 4, index // 2 % 4, index % 2
    where = jnp.stack([x, z * 4 + lax.axis_index("chan"), y * 2 + core, z]).astype(jnp.int32)
    pieces = split_features(where, layer_input)
    own = [lax.ppermute(pieces[n], "seq", along_x(n)) for n in range(1, 4)]
    own = jnp.stack([pieces[0]] + own)
    sent = gather_signals(gate_key, value_proj, grad_out, gate_query, filter_taps)
    up, down = ring_step(own, 1), ring_step(own, -1)
    tables = stage(tables)
    signals = exchange(sent)
    up2, down2 = ring_step(up, 1), ring_step(down, -1)
    back_grad, rest, *pieces = convolve(where, signals, tables)
    pieces = pieces[:1] + [lax.ppermute(pieces[n], "seq", across(2 * n)) for n in range(1, 4)]
    kept, sent = sort_cores(pieces)
    received = lax.ppermute(sent, "seq", across(1))
    up3, down3 = ring_step(up2, 1), ring_step(down2, -1)
    far = ring_step(up2, 2)
    results = complete(back_grad, rest, tables)
    value = bundle(kept, received)
    right, left = (lax.ppermute(value, "seq", along_x(n)) for n in (1, 3))
    values = [value, right, lax.ppermute(value, "seq", along_x(2)), left]
    results = exchange(results)
    kept, sent = weight_parts(where, values, (own, up, up2, up3, far, down3, down2, down))
    received = lax.ppermute(sent, "seq", across(1))
    parts = join_cores(kept, received)
    near = [lax.ppermute(parts[n], "seq", across(2 * n)) for n in (1, 3)]
    parts = [parts[0], lax.ppermute(parts[2], "seq", across(4)), *near]
    kept, sent = weight_total(where, parts)
    received = lax.ppermute(sent, "seq", opposite()).astype(jnp.float32)
    grad_query, grad_key, grad_value, grad_filter = finish(results, grad_out, value_proj, gate_key)
    grad_weight = jnp.where(
        z == 0,
        jnp.concatenate([kept, received], axis=1),
        jnp.concatenate([received, kept], axis=1),
    )
    return (grad_query, grad_key, grad_value, grad_filter, grad_weight)


def solution(mesh):
    placed = P("seq", "chan")
    return jax.shard_map(
        shards,
        mesh=mesh,
        in_specs=(placed,) * 6,
        out_specs=(placed,) * 5,
        check_vma=False,
    )
```
